128 devices in a mesh: skyx: 8 (over y, core), skyy: 16 (over x, z).
Axes of the slice: x: 4, y: 4, z: 4, core: 2. Of those that a mesh axis runs over, the one named last changes fastest.
Arguments:
- image: bfloat16 [8192, 16, 512], P(('skyx', 'skyy')), may hold values from -6 to 6
- inverse_var: bfloat16 [8192, 16, 512], P(('skyx', 'skyy')), may hold values from 0.099609375 to 1
- patch_of: int32 [8192, 1], replicated, may hold values from 0 to 127; in each aligned block of 64 rows (0 to 63, 64 to 127, ...) no two rows name the same one
- row_of: int32 [8192], replicated, may hold values from 0 to 3
- valid: int32 [8192], replicated, may hold values 0 or 1
- coef_index: int32 [128], replicated, may hold values from 0 to 63
- coef_table: float32 [64, 20], replicated, may hold values from -1.25 to 1.25
- basis_across: float32 [20, 41], replicated, may hold values from -1 to 1
- basis_down: float32 [20, 41], replicated, may hold values from -1 to 1
Outputs:
- coadd: float32 [1024, 4096], P('skyy', 'skyx')
- weight_sum: float32 [1024, 4096], P('skyy', 'skyx')
The draws below stay inside these ranges and needn't reach their ends.
Inputs may be any that keep to these rules, and one draw needn't show every extreme that they name: `patch_of`: within the 64 blocks of one exposure (the rows of one device) no patch appears twice.
All inputs are finite; a program needn't handle non-finite values.
Results may differ from the reference program's by a relative error of at most 0.0065.
Values may be sent and summed in bfloat16 or wider, within the bound.
No kernel may reach another device: no remote copies, remote signals or barrier semaphores. Data moves between devices by JAX's collectives and lax.ppermute only.
A program may use at most 192 MiB of HBM per device.

```python
import math
import jax
import jax.numpy as jnp
import numpy as np
from jax import lax

BW = 512
BR = 16
RS = 4
NCHAN = 20
TAPS = 41
NCOEF = 64
OUTW = 640
PR = 64
EXPOSURES = 128
NB = 64
BLOCKS = 8192
N_SKYX = 8
N_SKYY = 16


def plant(drawn, stream_key, smallest, largest):
    longest = drawn.shape.index(max(drawn.shape))
    spots = []
    for shift in (0, 1):
        where = [jax.random.randint(jax.random.fold_in(stream_key, axis), (), 0, length) for axis, length in enumerate(drawn.shape)]
        where[longest] = (where[longest] + shift) % drawn.shape[longest]
        spots.append(tuple(where))
    return drawn.at[spots[0]].set(smallest).at[spots[1]].set(largest)


def levels(own_key, shape, pieces, least, top_value):
    def one(dim, blocks):
        steps = jax.random.uniform(jax.random.fold_in(jax.random.fold_in(own_key, 6), dim), (blocks,), jnp.float32, least / len(pieces), top_value / len(pieces))
        return jnp.repeat(jnp.exp(steps), shape[dim] // blocks).reshape((-1,) + (1,) * (len(shape) - dim - 1))

    loudness = one(*pieces[0])
    for cut in pieces[1:]:
        loudness = loudness * one(*cut)
    return loudness


def routed_block(rng, own, number, rows, number_of, top, limit, lean):
    sequence = jax.random.permutation(rng, number_of)
    heavy_load, ordinary = portions_of(number_of, rows * top, limit, lean, True), portions_of(number_of, rows * top, limit, lean, False)
    places = jnp.arange(number_of)

    def named(sizes, offset_by):
        used = int((sizes > 0).sum())
        fixed = max(1, used // 4)
        moved = fixed + (places - fixed + offset_by * (used - fixed)) % max(1, number_of - fixed)
        return jnp.zeros((number_of,), jnp.int32).at[sequence[jnp.where(places < fixed, places, moved)]].set(jnp.asarray(sizes, jnp.int32))

    sizes = jnp.where(number % 4 == 0, named(heavy_load, number // 4), named(ordinary, number - number // 4 - 1))
    mixed = jax.random.permutation(jax.random.fold_in(own, 3), number_of)
    donor, sink = mixed[0:number_of // 2 * 2:2], mixed[1:number_of // 2 * 2:2]
    room = jnp.minimum(sizes[donor] - 1, limit - sizes[sink]) // 2
    room = jnp.where((donor == sequence[0]) | (sink == sequence[0]) | (sizes[sink] == 0), 0, jnp.maximum(room, 0))
    moved = jax.random.randint(jax.random.fold_in(own, 4), (number_of // 2,), 0, 1 << 20) % (room + 1)
    sizes = sizes.at[donor].add(-moved).at[sink].add(moved)
    items = jnp.searchsorted(jnp.cumsum(sizes), jnp.arange(rows * top), side="right").astype(jnp.int32)
    grid = items.reshape(top, rows).T
    grid = grid[jax.random.permutation(jax.random.fold_in(own, 1), rows)]
    offset_by = jax.random.randint(jax.random.fold_in(own, 2), (rows, 1), 0, top)
    return jnp.take_along_axis(grid, (jnp.arange(top)[None, :] + offset_by) % top, axis=1)


def portions_of(number_of, total, most, slope, full):
    weights = [(1 << 20) // math.isqrt(rank ** slope) + 1 for rank in range(1, number_of + 1)]
    largest = most if full else min(most, max(-(-total // number_of), total * weights[0] // sum(weights)))
    least = 1 if total - largest >= number_of - 1 else 0
    counts, spare = [largest] + [least] * (number_of - 1), total - largest - least * (number_of - 1)
    while spare > 0:
        candidates = [i for i in range(1, number_of) if counts[i] < largest] or [i for i in range(1, number_of) if counts[i] < most]
        mass, remaining = sum([weights[i] for i in candidates]), spare
        for i in candidates:
            more = min(most - counts[i], max(1, remaining * weights[i] // mass), spare)
            counts[i] = counts[i] + more
            spare = spare - more
    return np.array(counts)


def gaussian(stream_key, extent, spread, limit, split=(), kind=jnp.bfloat16):
    drawn = spread * jax.random.normal(stream_key, extent, jnp.float32)
    if split:
        drawn = drawn * levels(stream_key, extent, split, -0.22, 0.18)
    return jnp.clip(drawn, -limit, limit).astype(kind)


def setup_inputs(seed: int = 0) -> dict:
    key_list = jax.random.split(jax.random.key(seed), 10)
    image = gaussian(key_list[0], (BLOCKS, BR, BW), 1.0, 6.0, ((0, 128),))
    inverse_var = jnp.clip(jnp.exp(math.log(1.0) - 2.306499 * jax.random.uniform(key_list[1], (BLOCKS, BR, BW), jnp.float32) ** levels(key_list[1], (BLOCKS, BR, BW), ((0, 128),), -0.2, 0.2)), 0.099609375, 1.0).astype(jnp.bfloat16)
    patch_of_keys = jax.random.split(jax.random.fold_in(key_list[2], 1), BLOCKS // NB)
    patch_of_turns = jax.random.permutation(jax.random.fold_in(key_list[2], 3), BLOCKS // NB)
    patch_of = jax.vmap(lambda own, number: routed_block(jax.random.fold_in(key_list[2], 2), own, number, NB, EXPOSURES, 1, 1, 2))(patch_of_keys, patch_of_turns).reshape((BLOCKS, 1))
    row_of = plant(jax.random.randint(key_list[3], (BLOCKS,), 0, RS), jax.random.fold_in(key_list[3], 1), 0, RS - 1).astype(jnp.int32)
    valid = plant((jax.random.randint(key_list[4], (BLOCKS,), 0, 8) < 7).astype(jnp.int32), jax.random.fold_in(key_list[4], 1), 0, 1)
    coef_index = plant(jax.random.randint(key_list[5], (EXPOSURES,), 0, NCOEF), jax.random.fold_in(key_list[5], 1), 0, NCOEF - 1).astype(jnp.int32)
    coef_table = gaussian(key_list[6], (NCOEF, NCHAN), NCHAN ** -0.5, 1.25, (), jnp.float32)
    basis_across = gaussian(key_list[7], (NCHAN, TAPS), TAPS ** -0.5, 1.0, (), jnp.float32)
    basis_down = gaussian(key_list[8], (NCHAN, TAPS), TAPS ** -0.5, 1.0, (), jnp.float32)
    return {"image": image, "inverse_var": inverse_var, "patch_of": patch_of, "row_of": row_of, "valid": valid, "coef_index": coef_index, "coef_table": coef_table, "basis_across": basis_across, "basis_down": basis_down}


def across_matrix(basis_across):
    margin = (basis_across.shape[1] - 1) // 2
    rows_in = jnp.arange(128 + 2 * margin, dtype=jnp.int32)[:, None]
    cols_out = jnp.arange(128, dtype=jnp.int32)[None, :]
    offset = cols_out + 2 * margin - rows_in
    inside = (offset >= 0) & (offset <= 2 * margin)
    picked = jnp.take(basis_across, jnp.clip(offset, 0, 2 * margin), axis=1)
    return jnp.where(inside[None], picked, 0.0).astype(jnp.bfloat16)


def vertical_mix(basis_down, coeffs, row_count):
    margin = (basis_down.shape[1] - 1) // 2
    rows_out = jnp.arange(row_count + 2 * margin, dtype=jnp.int32)[:, None]
    rows_in = jnp.arange(row_count, dtype=jnp.int32)[None, :]
    offset = rows_out - rows_in
    inside = (offset >= 0) & (offset <= 2 * margin)
    picked = jnp.where(inside[None], jnp.take(basis_down, jnp.clip(offset, 0, 2 * margin), axis=1), 0.0)
    mixed_taps = coeffs[:, :, None, None] * picked[None]
    mixed_taps = jnp.transpose(mixed_taps, (0, 2, 1, 3))
    return mixed_taps.reshape(mixed_taps.shape[0], row_count + 2 * margin, -1).astype(jnp.bfloat16)


def convolve(planes, coeffs, across, basis_down, out_width):
    block_count, row_count, block_width = planes.shape
    margin = (basis_down.shape[1] - 1) // 2
    padded = jnp.pad(planes, ((0, 0), (0, 0), (2 * margin, out_width - block_width)))
    column_tiles = jnp.stack([padded[:, :, 128 * tile_index:128 * tile_index + 128 + 2 * margin] for tile_index in range(out_width // 128)], axis=1)
    swept_rows = jnp.einsum("ktri,cio->kcrto", column_tiles.astype(jnp.float32), across.astype(jnp.float32)).astype(jnp.bfloat16)
    swept_rows = swept_rows.reshape(block_count, -1, out_width)
    mixer_taps = vertical_mix(basis_down, coeffs, row_count)
    return jnp.einsum("kyj,kjx->kyx", mixer_taps.astype(jnp.float32), swept_rows.astype(jnp.float32)).astype(jnp.bfloat16)


def reference(image, inverse_var, patch_of, row_of, valid, coef_index, coef_table, basis_across, basis_down):
    margin = (TAPS - 1) // 2
    valid_flags = valid.astype(jnp.float32)[:, None, None]
    kept_planes = (valid_flags * inverse_var.astype(jnp.float32)).astype(jnp.bfloat16)
    weighted = (valid_flags * inverse_var.astype(jnp.float32) * image.astype(jnp.float32)).astype(jnp.bfloat16)
    choose = (coef_index[:, None] == jnp.arange(NCOEF, dtype=jnp.int32)[None, :]).astype(jnp.float32)
    coeffs = jnp.dot(choose, coef_table, precision=lax.Precision.HIGHEST)
    patch_ids = patch_of[:, 0]
    top_rows = ((patch_ids % N_SKYY) * PR + row_of * BR).astype(jnp.int32)
    left_cols = ((patch_ids // N_SKYY) * BW).astype(jnp.int32)
    across = across_matrix(basis_across)
    flux_sum = jnp.zeros((N_SKYY * PR + 2 * margin, N_SKYX * BW - BW + OUTW), jnp.float32)
    weight = jnp.zeros((N_SKYY * PR, N_SKYX * BW), jnp.float32)

    def per_exposure(state_in, inputs):
        planes, kept_rows, coef_row, tops_here, lefts_here = inputs
        rows_coef = jnp.broadcast_to(coef_row[None, :], (planes.shape[0], coef_row.shape[0]))
        contrib = convolve(planes, rows_coef, across, basis_down, OUTW)

        def place_one(position, state):
            flux_now, weight_now = state
            top_row = tops_here[position]
            left_col = lefts_here[position]
            window = lax.dynamic_slice(flux_now, (top_row, left_col), (contrib.shape[1], contrib.shape[2]))
            flux_now = lax.dynamic_update_slice(flux_now, window + contrib[position].astype(jnp.float32), (top_row, left_col))
            window = lax.dynamic_slice(weight_now, (top_row, left_col), (kept_rows.shape[1], kept_rows.shape[2]))
            weight_now = lax.dynamic_update_slice(weight_now, window + kept_rows[position].astype(jnp.float32), (top_row, left_col))
            return flux_now, weight_now

        return lax.fori_loop(0, planes.shape[0], place_one, state_in), None

    inputs = (weighted.reshape(EXPOSURES, NB, BR, BW), kept_planes.reshape(EXPOSURES, NB, BR, BW), coeffs,
              top_rows.reshape(EXPOSURES, NB), left_cols.reshape(EXPOSURES, NB))
    (flux_sum, weight), _ = lax.scan(per_exposure, (flux_sum, weight), inputs)
    return flux_sum[margin:margin + N_SKYY * PR, margin:margin + N_SKYX * BW], weight
```

```python
import functools

import jax
import jax.numpy as jnp
from jax import lax
from jax.experimental import pallas as pl
from jax.experimental.pallas import tpu as pltpu
from jax.sharding import PartitionSpec as P

RS = 4
LANES = 128
BOTH = ("skyx", "skyy")


def from_behind(value, axis, steps):
    count = lax.axis_size(axis)
    initial, last = (max(0, -steps), min(count, count - steps))
    return lax.ppermute(value, axis, [(source, source + steps) for source in range(initial, last)])


def pack_kernel(group, targets, valid, *refs):
    *planes, out, block_of = refs
    step = pl.program_id(0)
    blocks = targets.shape[0]

    @pl.when(step == 0)
    def _():
        @pl.loop(0, block_of.shape[0])
        def _(patch):
            block_of[patch] = -1

        @pl.loop(0, blocks)
        def _(block):
            block_of[targets[block]] = block

    @pl.loop(0, group)
    def _(offset):
        block = block_of[step * group + offset]
        at = jnp.maximum(block, 0)
        factor = jnp.where(block >= 0, valid[at], 0).astype(jnp.float32)
        value = factor * planes[0][at].astype(jnp.float32)
        for plane in planes[1:]:
            value = value * plane[at].astype(jnp.float32)
        out[offset] = value.astype(out.dtype)


def pack(devices, targets, valid, *planes):
    blocks, rows, width = planes[0].shape
    group = 16
    return pl.pallas_call(
        functools.partial(pack_kernel, group),
        out_shape=jax.ShapeDtypeStruct((devices, rows, width), jnp.bfloat16),
        grid_spec=pltpu.PrefetchScalarGridSpec(
            num_scalar_prefetch=2,
            grid=(devices // group,),
            in_specs=[
                pl.BlockSpec((blocks, rows, width), lambda step, *_: (0, 0, 0), pipeline_mode=pl.Buffered(1))
                for _ in planes
            ],
            out_specs=pl.BlockSpec((group, rows, width), lambda step, *_: (step, 0, 0)),
            scratch_shapes=[pltpu.SMEM((devices,), jnp.int32)],
        ),
        cost_estimate=pl.CostEstimate(
            flops=devices * rows * width,
            bytes_accessed=2 * (len(planes) * blocks + devices) * rows * width,
            transcendentals=0,
        ),
        name="pack",
    )(targets, valid, *planes)


def coadd_kernel(flux, choose, down, across, out, wide, channels, mixed):
    sources, rows, width = flux.shape
    count, ext, _ = down.shape
    tiles = out.shape[1] // LANES
    pieces = width // LANES
    for piece in range(pieces):
        lanes = pl.ds(piece * LANES, LANES)
        wide[piece] = flux[:, :, lanes].reshape(sources * rows, LANES).astype(jnp.float32)
    table = choose[...]
    for pair in range(rows // 2):
        halves = []
        for half in range(2):
            at = pl.ds(2 * pair + half, sources, stride=rows)
            row = [wide[piece, at, :].astype(jnp.bfloat16) for piece in range(pieces)]
            halves.append(jnp.concatenate(row, axis=1))
        summed = jnp.dot(table, jnp.concatenate(halves, axis=0), preferred_element_type=jnp.float32)
        channels[:, pair * 8 : pair * 8 + 8, :] = summed.reshape(count, 8, width)
    zeros = jnp.zeros((ext, LANES), jnp.bfloat16)
    for c in range(count):
        mixed[c, :, :LANES] = zeros
        mixed[c, :, LANES + width :] = zeros
        mixed[c, :, LANES : LANES + width] = jnp.dot(
            down[c], channels[c].astype(jnp.bfloat16), preferred_element_type=jnp.float32
        ).astype(jnp.bfloat16)
    total = jnp.zeros((tiles * ext, LANES), jnp.float32)
    for c in range(count):
        windows = jnp.concatenate([mixed[c, :, LANES * t : LANES * t + 2 * LANES] for t in range(tiles)], axis=0)
        total = total + jnp.dot(windows, across[c], preferred_element_type=jnp.float32)
    for t in range(tiles):
        out[:, t * LANES : (t + 1) * LANES] = total[t * ext : (t + 1) * ext]


def convolve_sum(flux, choose, down, across, out_width):
    sources, rows, width = flux.shape
    count, ext, _ = down.shape
    tiles = out_width // LANES
    return pl.pallas_call(
        coadd_kernel,
        out_shape=jax.ShapeDtypeStruct((ext, out_width), jnp.float32),
        in_specs=[pl.BlockSpec(memory_space=pltpu.VMEM)] * 4,
        out_specs=pl.BlockSpec(memory_space=pltpu.VMEM),
        scratch_shapes=[
            pltpu.VMEM((width // LANES, sources * rows, LANES), jnp.float32),
            pltpu.VMEM((count, RS * rows, width), jnp.float32),
            pltpu.VMEM((count, ext, (tiles + 1) * LANES), jnp.bfloat16),
        ],
        compiler_params=pltpu.CompilerParams(vmem_limit_bytes=40 << 20),
        cost_estimate=pl.CostEstimate(
            flops=2 * count * ext * out_width * 2 * LANES,
            bytes_accessed=2 * sources * rows * width + 4 * ext * out_width,
            transcendentals=0,
        ),
        name="convolve_sum",
    )(flux, choose, down, across)


def weight_kernel(slots, kept, out):
    step = pl.program_id(0)
    group, rows, _ = kept.shape

    @pl.when(step == 0)
    def _():
        out[...] = jnp.zeros_like(out)

    @pl.loop(0, group)
    def _(offset):
        slot = slots[step * group + offset]

        @pl.when(slot >= 0)
        def _():
            at = pl.ds(pl.multiple_of(slot * rows, rows), rows)
            out[at, :] += kept[offset].astype(jnp.float32)


def place_weights(slots, kept):
    sources, rows, width = kept.shape
    group = 32
    return pl.pallas_call(
        weight_kernel,
        out_shape=jax.ShapeDtypeStruct((RS * rows, width), jnp.float32),
        grid_spec=pltpu.PrefetchScalarGridSpec(
            num_scalar_prefetch=1,
            grid=(sources // group,),
            in_specs=[pl.BlockSpec((group, rows, width), lambda step, *_: (step, 0, 0))],
            out_specs=pl.BlockSpec((RS * rows, width), lambda step, *_: (0, 0)),
        ),
        cost_estimate=pl.CostEstimate(
            flops=sources * rows * width,
            bytes_accessed=2 * sources * rows * width,
            transcendentals=0,
        ),
        name="place_weights",
    )(slots, kept)


def spread(taps, offset):
    picked = jnp.zeros((taps.shape[0],) + offset.shape, jnp.float32)
    shape = (-1,) + (1,) * offset.ndim
    for tap in range(taps.shape[1]):
        picked = jnp.where(offset[None] == tap, taps[:, tap].reshape(shape), picked)
    return picked.astype(jnp.bfloat16)


def body(
    image, inverse_var, patch_of, row_of, valid, coef_index, coef_table, basis_across, basis_down
):
    devices = lax.axis_size("skyx") * lax.axis_size("skyy")
    block_count, row_count, block_width = image.shape
    channels = basis_across.shape[0]
    margin = (basis_across.shape[1] - 1) // 2
    out_width = (block_width + 2 * margin + 127) // 128 * 128
    patch_rows = RS * row_count
    ext = (patch_rows + 2 * margin + 15) // 16 * 16
    my_patch = lax.axis_index("skyx") * lax.axis_size("skyy") + lax.axis_index("skyy")
    first_row = my_patch * block_count
    patches = patch_of[:, 0]
    my_valid = lax.dynamic_slice_in_dim(valid, first_row, block_count)
    my_targets = lax.dynamic_slice_in_dim(patches, first_row, block_count)

    weighted_in = lax.all_to_all(
        pack(devices, my_targets, my_valid, inverse_var, image), BOTH, split_axis=0, concat_axis=0, tiled=True
    )
    kept_in = lax.all_to_all(
        pack(devices, my_targets, my_valid, inverse_var), BOTH, split_axis=0, concat_axis=0, tiled=True
    )

    choose = (
        coef_index[:, None] == jnp.arange(coef_table.shape[0], dtype=jnp.int32)[None, :]
    ).astype(jnp.float32)
    coeffs = jnp.dot(choose, coef_table, precision=lax.Precision.HIGHEST)
    target_grid = patches.reshape(devices, block_count)
    slot_grid = row_of.reshape(devices, block_count)
    hits = target_grid == my_patch
    slot = jnp.max(jnp.where(hits, slot_grid, -1), axis=1)
    in_slot = slot[None, :] == jnp.arange(RS, dtype=jnp.int32)[:, None]
    one = jnp.where(in_slot[None], coeffs.T[:, None, :], 0.0)
    none = jnp.zeros_like(one)
    table = jnp.concatenate(
        [jnp.concatenate([one, none], axis=2), jnp.concatenate([none, one], axis=2)], axis=1
    ).reshape(channels * 2 * RS, 2 * devices).astype(jnp.bfloat16)
    places = jnp.arange(patch_rows, dtype=jnp.int32)
    row_at = (places % RS) * row_count + places // RS
    down = spread(basis_down, jnp.arange(ext, dtype=jnp.int32)[:, None] - row_at[None, :])
    across = spread(
        basis_across,
        jnp.arange(LANES, dtype=jnp.int32)[None, :] + LANES - jnp.arange(2 * LANES, dtype=jnp.int32)[:, None],
    )
    extended = convolve_sum(weighted_in, table, down, across, out_width)

    from_below = from_behind(extended[:margin], "skyy", -1)
    from_above = from_behind(extended[patch_rows + margin : patch_rows + 2 * margin], "skyy", 1)
    middle = extended[margin : margin + patch_rows]
    middle = middle.at[patch_rows - margin :].add(from_below)
    middle = middle.at[:margin].add(from_above)
    right_start = min(block_width + margin, out_width - 128)
    right_offset = block_width + margin - right_start
    from_right = from_behind(middle[:, :128], "skyx", -1)
    from_left = from_behind(middle[:, right_start : right_start + 128], "skyx", 1)
    coadd = middle[:, margin : margin + block_width]
    coadd = coadd.at[:, block_width - margin :].add(from_right[:, :margin])
    coadd = coadd.at[:, :margin].add(from_left[:, right_offset : right_offset + margin])
    weight_sum = place_weights(slot, kept_in)
    return (coadd, weight_sum)


def solution(mesh):
    placed = (P(BOTH, None, None), P(BOTH, None, None), P(), P(), P(), P(), P(), P(), P())
    return jax.shard_map(
        body,
        mesh=mesh,
        in_specs=placed,
        out_specs=(P("skyy", "skyx"), P("skyy", "skyx")),
        check_vma=False,
    )
```

```python
import functools

import jax
import jax.numpy as jnp
from jax import lax
from jax.experimental import pallas as pl
from jax.experimental.pallas import tpu as pltpu
from jax.sharding import PartitionSpec as P

RS = 4
LANES = 128
BOTH = ("skyx", "skyy")


def from_behind(value, axis, steps):
    count = lax.axis_size(axis)
    initial, last = (max(0, -steps), min(count, count - steps))
    return lax.ppermute(value, axis, [(source, source + steps) for source in range(initial, last)])


def pack_kernel(planes, me, patch_of, valid, *refs):
    sources, refs = refs[:planes], refs[planes:]
    out, *rooms, packed, targets, usable, arrived, noted, sent = refs
    blocks = rooms[0].shape[0]
    chunks = arrived.shape[1]
    group = blocks // chunks

    def fetch(index, chunk):
        at = pl.ds(chunk * group, group)
        return pltpu.make_async_copy(sources[index].at[at], rooms[index].at[at], arrived.at[index, chunk])

    notes = [pltpu.make_async_copy(patch_of, targets, noted.at[0]), pltpu.make_async_copy(valid, usable, noted.at[1])]
    for note in notes:
        note.start()
    for chunk in range(chunks):
        for index in range(planes):
            fetch(index, chunk).start()
    packed[...] = jnp.zeros_like(packed)
    for note in notes:
        note.wait()
    first = me[0] * blocks
    for chunk in range(chunks):
        for index in range(planes):
            fetch(index, chunk).wait()
        for block in range(chunk * group, chunk * group + group):
            value = rooms[0][block]
            for room in rooms[1:]:
                value = value * room[block]
            place = targets[first + block]
            packed[place] = jnp.where(usable[first + block] != 0, value, jnp.zeros_like(value))
    pieces = sent.shape[0]
    share = packed.shape[0] // pieces
    copies = []
    for piece in range(pieces):
        at = pl.ds(piece * share, share)
        copies.append(pltpu.make_async_copy(packed.at[at], out.at[at], sent.at[piece]))
        copies[-1].start()
    for copy in copies:
        copy.wait()


def pack(devices, me, patch_of, valid, *planes):
    blocks, rows, width = planes[0].shape
    chunks, pieces = 4, 8
    return pl.pallas_call(
        functools.partial(pack_kernel, len(planes)),
        out_shape=jax.ShapeDtypeStruct((devices, rows, width), jnp.bfloat16),
        in_specs=[pl.BlockSpec(memory_space=pltpu.SMEM)] + [pl.BlockSpec(memory_space=pl.ANY)] * (2 + len(planes)),
        out_specs=pl.BlockSpec(memory_space=pl.ANY),
        scratch_shapes=[pltpu.VMEM((blocks, rows, width), jnp.bfloat16) for _ in planes]
        + [
            pltpu.VMEM((devices, rows, width), jnp.bfloat16),
            pltpu.SMEM(patch_of.shape, jnp.int32),
            pltpu.SMEM(valid.shape, jnp.int32),
            pltpu.SemaphoreType.DMA((len(planes), chunks)),
            pltpu.SemaphoreType.DMA((2,)),
            pltpu.SemaphoreType.DMA((pieces,)),
        ],
        cost_estimate=pl.CostEstimate(
            flops=devices * rows * width,
            bytes_accessed=2 * (len(planes) * blocks + devices) * rows * width,
            transcendentals=0,
        ),
        name="pack",
    )(me, patch_of, valid, *planes)


def table_kernel(across_taps, down_taps, row_at, across, down):
    count, ext, places = down.shape
    lane = lax.broadcasted_iota(jnp.int32, (LANES, LANES), 1)
    line = lax.broadcasted_iota(jnp.int32, (LANES, LANES), 0)
    order = (lax.broadcasted_iota(jnp.int32, (LANES, places), 0) == row_at[...]).astype(jnp.bfloat16)
    for c in range(count):
        turned = jnp.broadcast_to(across_taps[c : c + 1, :], (LANES, LANES))
        turned = pltpu.roll(turned, 0, 1, stride=1, stride_axis=0)
        across[c, LANES:, :] = jnp.where(lane >= line, turned, 0.0).astype(jnp.bfloat16)
        across[c, :LANES, :] = jnp.where(lane < line, turned, 0.0).astype(jnp.bfloat16)
        turned = jnp.broadcast_to(down_taps[c : c + 1, :], (LANES, LANES))
        turned = pltpu.roll(turned, 0, 1, stride=1, stride_axis=0)[:ext].astype(jnp.bfloat16)
        down[c] = jnp.dot(turned, order, preferred_element_type=jnp.float32).astype(jnp.bfloat16)


def band_tables(basis_across, basis_down, row_at, ext):
    channels, taps = basis_across.shape
    places = row_at.shape[1]
    across_taps = jnp.pad(basis_across, ((0, 0), (0, LANES - taps)))
    down_taps = jnp.concatenate(
        [basis_down[:, :1], jnp.zeros((channels, LANES - taps), jnp.float32), basis_down[:, :0:-1]], axis=1
    )
    return pl.pallas_call(
        table_kernel,
        out_shape=(
            jax.ShapeDtypeStruct((channels, 2 * LANES, LANES), jnp.bfloat16),
            jax.ShapeDtypeStruct((channels, ext, places), jnp.bfloat16),
        ),
        in_specs=[pl.BlockSpec(memory_space=pltpu.VMEM)] * 3,
        out_specs=(pl.BlockSpec(memory_space=pltpu.VMEM),) * 2,
        compiler_params=pltpu.CompilerParams(vmem_limit_bytes=8 << 20),
        name="band_tables",
    )(across_taps, down_taps, row_at)


def coadd_kernel(margin, flux, choose, down, across, inner, top, bottom, wide, channels, mixed):
    sources, rows, width = flux.shape
    count, ext, _ = down.shape
    pieces = width // LANES
    tiles = pieces + 1
    edge = top.shape[0]
    tall = inner.shape[0]
    for piece in range(pieces):
        lanes = pl.ds(piece * LANES, LANES)
        wide[piece] = flux[:, :, lanes].reshape(sources * rows, LANES).astype(jnp.float32)
    table = choose[...]
    for pair in range(rows // 2):
        halves = []
        for half in range(2):
            at = pl.ds(2 * pair + half, sources, stride=rows)
            row = [wide[piece, at, :].astype(jnp.bfloat16) for piece in range(pieces)]
            halves.append(jnp.concatenate(row, axis=1))
        summed = jnp.dot(table, jnp.concatenate(halves, axis=0), preferred_element_type=jnp.float32)
        channels[:, pair * 8 : pair * 8 + 8, :] = summed.reshape(count, 8, width)
    zeros = jnp.zeros((ext, LANES), jnp.bfloat16)
    for c in range(count):
        mixed[c, :, :LANES] = zeros
        mixed[c, :, LANES + width :] = zeros
        mixed[c, :, LANES : LANES + width] = jnp.dot(
            down[c], channels[c].astype(jnp.bfloat16), preferred_element_type=jnp.float32
        ).astype(jnp.bfloat16)
    total = jnp.zeros((tiles * ext, LANES), jnp.float32)
    for c in range(count):
        windows = jnp.concatenate([mixed[c, :, LANES * t : LANES * t + 2 * LANES] for t in range(tiles)], axis=0)
        total = total + jnp.dot(windows, across[c], preferred_element_type=jnp.float32)
    whole = jnp.concatenate([total[t * ext : (t + 1) * ext] for t in range(tiles)], axis=1)
    whole = pltpu.roll(whole, tiles * LANES - margin, 1)
    top[...] = whole[:edge]
    inner[...] = whole[edge : edge + tall]
    bottom[...] = whole[edge + tall :]


def convolve_sum(margin, flux, choose, down, across):
    sources, rows, width = flux.shape
    count, ext, _ = down.shape
    tiles = width // LANES + 1
    tall = RS * rows
    edge = (ext - tall) // 2
    sizes = [(tall, tiles * LANES), (edge, tiles * LANES), (edge, tiles * LANES)]
    return pl.pallas_call(
        functools.partial(coadd_kernel, margin),
        out_shape=tuple(jax.ShapeDtypeStruct(size, jnp.float32) for size in sizes),
        in_specs=[pl.BlockSpec(memory_space=pltpu.VMEM)] * 4,
        out_specs=(pl.BlockSpec(memory_space=pltpu.VMEM),) * len(sizes),
        scratch_shapes=[
            pltpu.VMEM((width // LANES, sources * rows, LANES), jnp.float32),
            pltpu.VMEM((count, RS * rows, width), jnp.float32),
            pltpu.VMEM((count, ext, (tiles + 1) * LANES), jnp.bfloat16),
        ],
        compiler_params=pltpu.CompilerParams(vmem_limit_bytes=20 << 20),
        cost_estimate=pl.CostEstimate(
            flops=2 * count * ext * tiles * LANES * 2 * LANES,
            bytes_accessed=2 * sources * rows * width + 4 * ext * tiles * LANES,
            transcendentals=0,
        ),
        name="convolve_sum",
    )(flux, choose, down, across)


def weight_kernel(row_in_patch, kept, out):
    sources, rows, width = kept.shape
    line = lax.broadcasted_iota(jnp.int32, (out.shape[0], sources * rows), 0)
    chosen = (line == row_in_patch[...]).astype(jnp.bfloat16)
    out[...] = jnp.dot(chosen, kept[...].reshape(sources * rows, width), preferred_element_type=jnp.float32)


def place_weights(row_in_patch, kept):
    sources, rows, width = kept.shape
    return pl.pallas_call(
        weight_kernel,
        out_shape=jax.ShapeDtypeStruct((RS * rows, width), jnp.float32),
        in_specs=[pl.BlockSpec(memory_space=pltpu.VMEM)] * 2,
        out_specs=pl.BlockSpec(memory_space=pltpu.VMEM),
        compiler_params=pltpu.CompilerParams(vmem_limit_bytes=8 << 20),
        cost_estimate=pl.CostEstimate(
            flops=2 * RS * rows * sources * rows * width,
            bytes_accessed=2 * sources * rows * width,
            transcendentals=0,
        ),
        name="place_weights",
    )(row_in_patch, kept)


def side_kernel(side, top, bottom, out):
    tall, _ = side.shape
    edge = top.shape[0]
    out[:edge, :] = side[:edge, :] + top[...]
    out[edge : tall - edge, :] = side[edge : tall - edge, :]
    out[tall - edge :, :] = side[tall - edge :, :] + bottom[...]


def add_beside(inner, top, bottom):
    tall, wide = inner.shape
    edge = top.shape[0]
    last = wide // LANES - 1
    return pl.pallas_call(
        side_kernel,
        out_shape=jax.ShapeDtypeStruct((tall, LANES), jnp.float32),
        grid=(1,),
        in_specs=[pl.BlockSpec((size, LANES), lambda step: (0, last)) for size in (tall, edge, edge)],
        out_specs=pl.BlockSpec((tall, LANES), lambda step: (0, 0)),
        compiler_params=pltpu.CompilerParams(vmem_limit_bytes=4 << 20),
        name="add_beside",
    )(inner, top, bottom)


def finish_kernel(margin, inner, top, bottom, left, right, out):
    tall, width = out.shape
    edge = top.shape[0]
    lane = lax.broadcasted_iota(jnp.int32, (1, LANES), 1)
    out[:edge, :] = inner[:edge, :width] + top[:, :width]
    out[edge : tall - edge, :] = inner[edge : tall - edge, :width]
    out[tall - edge :, :] = inner[tall - edge :, :width] + bottom[:, :width]
    out[:, :LANES] += jnp.where(lane < margin, left[...], 0.0)
    out[:, width - LANES :] += jnp.where(lane >= LANES - margin, right[...], 0.0)


def finish(margin, inner, top, bottom, left, right):
    tall, wide = inner.shape
    return pl.pallas_call(
        functools.partial(finish_kernel, margin),
        out_shape=jax.ShapeDtypeStruct((tall, wide - LANES), jnp.float32),
        in_specs=[pl.BlockSpec(memory_space=pltpu.VMEM)] * 5,
        out_specs=pl.BlockSpec(memory_space=pltpu.VMEM),
        compiler_params=pltpu.CompilerParams(vmem_limit_bytes=4 << 20),
        name="finish",
    )(inner, top, bottom, left, right)


def body(
    image, inverse_var, patch_of, row_of, valid, coef_index, coef_table, basis_across, basis_down
):
    devices = lax.axis_size("skyx") * lax.axis_size("skyy")
    block_count, row_count, block_width = image.shape
    channels = basis_across.shape[0]
    margin = (basis_across.shape[1] - 1) // 2
    patch_rows = RS * row_count
    columns, lines = lax.axis_size("skyx"), lax.axis_size("skyy")
    my_column, my_line = lax.axis_index("skyx"), lax.axis_index("skyy")
    my_patch = my_column * lines + my_line
    patches = patch_of[:, 0]
    me = my_patch.astype(jnp.int32).reshape(1)

    weighted = pack(devices, me, patches, valid, inverse_var, image)
    weighted_in = lax.all_to_all(weighted, BOTH, split_axis=0, concat_axis=0, tiled=True)
    kept = pack(devices, me, patches, valid, inverse_var)

    choose = (
        coef_index[:, None] == jnp.arange(coef_table.shape[0], dtype=jnp.int32)[None, :]
    ).astype(jnp.float32)
    coeffs = jnp.dot(choose, coef_table, precision=lax.Precision.HIGHEST)
    target_grid = patches.reshape(devices, block_count)
    slot_grid = row_of.reshape(devices, block_count)
    hits = target_grid == my_patch
    slot = jnp.max(jnp.where(hits, slot_grid, -1), axis=1)
    in_slot = slot[None, :] == jnp.arange(RS, dtype=jnp.int32)[:, None]
    one = jnp.where(in_slot[None], coeffs.T[:, None, :], 0.0)
    none = jnp.zeros_like(one)
    table = jnp.concatenate(
        [jnp.concatenate([one, none], axis=2), jnp.concatenate([none, one], axis=2)], axis=1
    ).reshape(channels * 2 * RS, 2 * devices).astype(jnp.bfloat16)
    places = jnp.arange(patch_rows, dtype=jnp.int32)
    edge = (margin + 7) // 8 * 8
    row_at = (places % RS) * row_count + places // RS + edge - margin
    across, down = band_tables(basis_across, basis_down, row_at[None, :], patch_rows + 2 * edge)
    received_rows = jnp.arange(row_count, dtype=jnp.int32)[None, :]
    row_in_patch = jnp.where(slot[:, None] >= 0, slot[:, None] * row_count + received_rows, -1)
    row_in_patch = row_in_patch.reshape(1, devices * row_count)
    kept, table, down, across, row_in_patch = lax.optimization_barrier((kept, table, down, across, row_in_patch))
    kept_in = lax.all_to_all(kept, BOTH, split_axis=0, concat_axis=0, tiled=True)
    inner, top, bottom = convolve_sum(margin, weighted_in, table, down, across)
    top, bottom = from_behind(bottom, "skyy", 1), from_behind(top, "skyy", -1)
    side = add_beside(inner, top, bottom)
    left, right = from_behind(side, "skyx", 1), from_behind(side, "skyx", -1)
    weight_sum = place_weights(row_in_patch, kept_in)
    coadd = finish(margin, inner, top, bottom, left, right)
    return (coadd, weight_sum)


def solution(mesh):
    placed = (P(BOTH, None, None), P(BOTH, None, None), P(), P(), P(), P(), P(), P(), P())
    return jax.shard_map(
        body,
        mesh=mesh,
        in_specs=placed,
        out_specs=(P("skyy", "skyx"), P("skyy", "skyx")),
        check_vma=False,
    )
```

```python
import functools

import jax
import jax.numpy as jnp
from jax import lax
from jax.experimental import pallas as pl
from jax.experimental.pallas import tpu as pltpu
from jax.sharding import PartitionSpec as P

RS = 4
LANES = 128
BOTH = ("skyx", "skyy")


def pack_kernel(planes, me, patch_of, valid, *refs):
    sources, refs = refs[:planes], refs[planes:]
    out, *rooms, packed, targets, usable, arrived, noted, sent = refs
    blocks = rooms[0].shape[0]
    chunks = arrived.shape[1]
    group = blocks // chunks

    def fetch(index, chunk):
        at = pl.ds(chunk * group, group)
        return pltpu.make_async_copy(sources[index].at[at], rooms[index].at[at], arrived.at[index, chunk])

    notes = [pltpu.make_async_copy(patch_of, targets, noted.at[0]), pltpu.make_async_copy(valid, usable, noted.at[1])]
    for note in notes:
        note.start()
    for chunk in range(chunks):
        for index in range(planes):
            fetch(index, chunk).start()
    packed[...] = jnp.zeros_like(packed)
    for note in notes:
        note.wait()
    first = me[0] * blocks
    for chunk in range(chunks):
        for index in range(planes):
            fetch(index, chunk).wait()
        for block in range(chunk * group, chunk * group + group):
            value = rooms[0][block]
            for room in rooms[1:]:
                value = value * room[block]
            place = targets[first + block]
            packed[place] = jnp.where(usable[first + block] != 0, value, jnp.zeros_like(value))
    pieces = sent.shape[0]
    share = packed.shape[0] // pieces
    copies = []
    for piece in range(pieces):
        at = pl.ds(piece * share, share)
        copies.append(pltpu.make_async_copy(packed.at[at], out.at[at], sent.at[piece]))
        copies[-1].start()
    for copy in copies:
        copy.wait()


def pack(devices, me, patch_of, valid, *planes):
    blocks, rows, width = planes[0].shape
    chunks, pieces = 4, 8
    return pl.pallas_call(
        functools.partial(pack_kernel, len(planes)),
        out_shape=jax.ShapeDtypeStruct((devices, rows, width), jnp.bfloat16),
        in_specs=[pl.BlockSpec(memory_space=pltpu.SMEM)] + [pl.BlockSpec(memory_space=pl.ANY)] * (2 + len(planes)),
        out_specs=pl.BlockSpec(memory_space=pl.ANY),
        scratch_shapes=[pltpu.VMEM((blocks, rows, width), jnp.bfloat16) for _ in planes]
        + [
            pltpu.VMEM((devices, rows, width), jnp.bfloat16),
            pltpu.SMEM(patch_of.shape, jnp.int32),
            pltpu.SMEM(valid.shape, jnp.int32),
            pltpu.SemaphoreType.DMA((len(planes), chunks)),
            pltpu.SemaphoreType.DMA((2,)),
            pltpu.SemaphoreType.DMA((pieces,)),
        ],
        cost_estimate=pl.CostEstimate(
            flops=devices * rows * width,
            bytes_accessed=2 * (len(planes) * blocks + devices) * rows * width,
            transcendentals=0,
        ),
        compiler_params=pltpu.CompilerParams(vmem_limit_bytes=63 << 20),
        name="pack",
    )(me, patch_of, valid, *planes)


def table_kernel(across_taps, down_taps, row_at, across, down):
    count, ext, places = down.shape
    lane = lax.broadcasted_iota(jnp.int32, (LANES, LANES), 1)
    line = lax.broadcasted_iota(jnp.int32, (LANES, LANES), 0)
    order = (lax.broadcasted_iota(jnp.int32, (LANES, places), 0) == row_at[...]).astype(jnp.bfloat16)
    for c in range(count):
        turned = jnp.broadcast_to(across_taps[c : c + 1, :], (LANES, LANES))
        turned = pltpu.roll(turned, 0, 1, stride=1, stride_axis=0)
        across[c, LANES:, :] = jnp.where(lane >= line, turned, 0.0).astype(jnp.bfloat16)
        across[c, :LANES, :] = jnp.where(lane < line, turned, 0.0).astype(jnp.bfloat16)
        turned = jnp.broadcast_to(down_taps[c : c + 1, :], (LANES, LANES))
        turned = pltpu.roll(turned, 0, 1, stride=1, stride_axis=0)[:ext].astype(jnp.bfloat16)
        down[c] = jnp.dot(turned, order, preferred_element_type=jnp.float32).astype(jnp.bfloat16)


def band_tables(basis_across, basis_down, row_at, ext):
    channels, taps = basis_across.shape
    places = row_at.shape[1]
    across_taps = jnp.pad(basis_across, ((0, 0), (0, LANES - taps)))
    down_taps = jnp.concatenate(
        [basis_down[:, :1], jnp.zeros((channels, LANES - taps), jnp.float32), basis_down[:, :0:-1]], axis=1
    )
    return pl.pallas_call(
        table_kernel,
        out_shape=(
            jax.ShapeDtypeStruct((channels, 2 * LANES, LANES), jnp.bfloat16),
            jax.ShapeDtypeStruct((channels, ext, places), jnp.bfloat16),
        ),
        in_specs=[pl.BlockSpec(memory_space=pltpu.VMEM)] * 3,
        out_specs=(pl.BlockSpec(memory_space=pltpu.VMEM),) * 2,
        compiler_params=pltpu.CompilerParams(vmem_limit_bytes=8 << 20),
        name="band_tables",
    )(across_taps, down_taps, row_at)


def coadd_kernel(
    margin, here, flux_far, choose, down_far, across_far, inner, first, second,
    flux, down, across, wide, channels, mixed, arrived,
):
    sources, rows, width = flux.shape
    count, ext, _ = down.shape
    pieces = width // LANES
    tiles = pieces + 1
    edge = first.shape[0]
    tall = inner.shape[0]
    chunks = arrived.shape[0] - 2
    share = sources // chunks
    copies = []
    for chunk in range(chunks):
        some = pl.ds(chunk * share, share)
        copies.append(pltpu.make_async_copy(flux_far.at[some], flux.at[some], arrived.at[chunk]))
    copies.append(pltpu.make_async_copy(down_far, down, arrived.at[chunks]))
    copies.append(pltpu.make_async_copy(across_far, across, arrived.at[chunks + 1]))
    for copy in copies:
        copy.start()
    for chunk in range(chunks):
        copies[chunk].wait()
        some = pl.ds(chunk * share, share)
        for piece in range(pieces):
            lanes = pl.ds(piece * LANES, LANES)
            block = flux[some, :, lanes].reshape(share * rows, LANES)
            wide[piece, pl.ds(chunk * share * rows, share * rows), :] = block.astype(jnp.float32)
    table = choose[...]
    for pair in range(rows // 2):
        halves = []
        for half in range(2):
            at = pl.ds(2 * pair + half, sources, stride=rows)
            row = [wide[piece, at, :].astype(jnp.bfloat16) for piece in range(pieces)]
            halves.append(jnp.concatenate(row, axis=1))
        summed = jnp.dot(table, jnp.concatenate(halves, axis=0), preferred_element_type=jnp.float32)
        channels[:, pair * 8 : pair * 8 + 8, :] = summed.reshape(count, 8, width)
    copies[chunks].wait()
    copies[chunks + 1].wait()
    zeros = jnp.zeros((ext, LANES), jnp.bfloat16)
    for c in range(count):
        mixed[c, :, :LANES] = zeros
        mixed[c, :, LANES + width :] = zeros
        mixed[c, :, LANES : LANES + width] = jnp.dot(
            down[c], channels[c].astype(jnp.bfloat16), preferred_element_type=jnp.float32
        ).astype(jnp.bfloat16)
    total = jnp.zeros((tiles * ext, LANES), jnp.float32)
    for c in range(count):
        windows = jnp.concatenate([mixed[c, :, LANES * t : LANES * t + 2 * LANES] for t in range(tiles)], axis=0)
        total = total + jnp.dot(windows, across[c], preferred_element_type=jnp.float32)
    whole = jnp.concatenate([total[t * ext : (t + 1) * ext] for t in range(tiles)], axis=1)
    whole = pltpu.roll(whole, tiles * LANES - margin, 1)
    inner[...] = whole[edge : edge + tall]
    top, bottom = whole[:edge], whole[edge + tall :]
    even = lax.rem(here[1], 2) == 0
    first[...] = jnp.where(even, bottom, top)
    second[...] = jnp.where(even, top, bottom)


def convolve_sum(margin, at, flux, choose, down, across):
    sources, rows, width = flux.shape
    count, ext, _ = down.shape
    tiles = width // LANES + 1
    tall = RS * rows
    edge = (ext - tall) // 2
    sizes = [(tall, tiles * LANES), (edge, tiles * LANES), (edge, tiles * LANES)]
    return pl.pallas_call(
        functools.partial(coadd_kernel, margin),
        out_shape=tuple(jax.ShapeDtypeStruct(size, jnp.float32) for size in sizes),
        in_specs=[
            pl.BlockSpec(memory_space=pltpu.SMEM),
            pl.BlockSpec(memory_space=pltpu.HBM),
            pl.BlockSpec(memory_space=pltpu.VMEM),
            pl.BlockSpec(memory_space=pltpu.HBM),
            pl.BlockSpec(memory_space=pltpu.HBM),
        ],
        out_specs=(pl.BlockSpec(memory_space=pltpu.VMEM),) * len(sizes),
        scratch_shapes=[
            pltpu.VMEM(flux.shape, jnp.bfloat16),
            pltpu.VMEM(down.shape, jnp.bfloat16),
            pltpu.VMEM(across.shape, jnp.bfloat16),
            pltpu.VMEM((width // LANES, sources * rows, LANES), jnp.float32),
            pltpu.VMEM((count, RS * rows, width), jnp.float32),
            pltpu.VMEM((count, ext, (tiles + 1) * LANES), jnp.bfloat16),
            pltpu.SemaphoreType.DMA((4 + 2,)),
        ],
        compiler_params=pltpu.CompilerParams(vmem_limit_bytes=20 << 20),
        cost_estimate=pl.CostEstimate(
            flops=2 * count * ext * tiles * LANES * 2 * LANES,
            bytes_accessed=2 * sources * rows * width + 4 * ext * tiles * LANES,
            transcendentals=0,
        ),
        name="convolve_sum",
    )(at, flux, choose, down, across)


def weight_kernel(row_in_patch, kept, out):
    sources, rows, width = kept.shape
    line = lax.broadcasted_iota(jnp.int32, (out.shape[0], sources * rows), 0)
    chosen = (line == row_in_patch[...]).astype(jnp.bfloat16)
    out[...] = jnp.dot(chosen, kept[...].reshape(sources * rows, width), preferred_element_type=jnp.float32)


def place_weights(row_in_patch, kept):
    sources, rows, width = kept.shape
    return pl.pallas_call(
        weight_kernel,
        out_shape=jax.ShapeDtypeStruct((RS * rows, width), jnp.float32),
        in_specs=[pl.BlockSpec(memory_space=pltpu.VMEM)] * 2,
        out_specs=pl.BlockSpec(memory_space=pltpu.VMEM),
        compiler_params=pltpu.CompilerParams(vmem_limit_bytes=8 << 20),
        cost_estimate=pl.CostEstimate(
            flops=2 * RS * rows * sources * rows * width,
            bytes_accessed=2 * sources * rows * width,
            transcendentals=0,
        ),
        name="place_weights",
    )(row_in_patch, kept)


def by_parity(place, first, second):
    even = lax.rem(place, 2) == 0
    return jnp.where(even, second, first), jnp.where(even, first, second)


def side_kernel(at, inner, first, second, out):
    tall, wide = inner.shape
    edge = first.shape[0]
    lanes = slice(wide - LANES, wide)
    above, below = by_parity(at[1], first[:, lanes], second[:, lanes])
    out[:edge, :] = inner[:edge, lanes] + above
    out[edge : tall - edge, :] = inner[edge : tall - edge, lanes]
    out[tall - edge :, :] = inner[tall - edge :, lanes] + below


def add_beside(at, inner, first, second):
    return pl.pallas_call(
        side_kernel,
        out_shape=jax.ShapeDtypeStruct((inner.shape[0], LANES), jnp.float32),
        in_specs=[pl.BlockSpec(memory_space=pltpu.SMEM)] + [pl.BlockSpec(memory_space=pltpu.VMEM)] * 3,
        out_specs=pl.BlockSpec(memory_space=pltpu.VMEM),
        compiler_params=pltpu.CompilerParams(vmem_limit_bytes=4 << 20),
        name="add_beside",
    )(at, inner, first, second)


def finish_kernel(margin, at, inner, first, second, near, far, out):
    tall, width = out.shape
    edge = first.shape[0]
    above, below = by_parity(at[1], first[:, :width], second[:, :width])
    out[:edge, :] = inner[:edge, :width] + above
    out[edge : tall - edge, :] = inner[edge : tall - edge, :width]
    out[tall - edge :, :] = inner[tall - edge :, :width] + below
    lane = lax.broadcasted_iota(jnp.int32, (1, LANES), 1)
    left, right = by_parity(at[0], near[...], far[...])
    out[:, :LANES] += jnp.where(lane < margin, left, 0.0)
    out[:, width - LANES :] += jnp.where(lane >= LANES - margin, right, 0.0)


def finish(margin, at, inner, first, second, near, far):
    tall, wide = inner.shape
    return pl.pallas_call(
        functools.partial(finish_kernel, margin),
        out_shape=jax.ShapeDtypeStruct((tall, wide - LANES), jnp.float32),
        in_specs=[pl.BlockSpec(memory_space=pltpu.SMEM)] + [pl.BlockSpec(memory_space=pltpu.VMEM)] * 5,
        out_specs=pl.BlockSpec(memory_space=pltpu.VMEM),
        compiler_params=pltpu.CompilerParams(vmem_limit_bytes=4 << 20),
        name="finish",
    )(at, inner, first, second, near, far)


def swap(value, axis, first):
    pairs = [(i, i + 1) for i in range(first, lax.axis_size(axis) - 1, 2)]
    return lax.ppermute(value, axis, pairs + [(j, i) for i, j in pairs])


def body(
    image, inverse_var, patch_of, row_of, valid, coef_index, coef_table, basis_across, basis_down
):
    devices = lax.axis_size("skyx") * lax.axis_size("skyy")
    block_count, row_count, block_width = image.shape
    channels = basis_across.shape[0]
    margin = (basis_across.shape[1] - 1) // 2
    patch_rows = RS * row_count
    columns, lines = lax.axis_size("skyx"), lax.axis_size("skyy")
    my_column, my_line = lax.axis_index("skyx"), lax.axis_index("skyy")
    my_patch = my_column * lines + my_line
    patches = patch_of[:, 0]
    me = my_patch.astype(jnp.int32).reshape(1)

    weighted = pack(devices, me, patches, valid, inverse_var, image)
    weighted_in = lax.all_to_all(weighted, BOTH, split_axis=0, concat_axis=0, tiled=True)
    kept = pack(devices, me, patches, valid, inverse_var)

    choose = (
        coef_index[:, None] == jnp.arange(coef_table.shape[0], dtype=jnp.int32)[None, :]
    ).astype(jnp.float32)
    coeffs = jnp.dot(choose, coef_table, precision=lax.Precision.HIGHEST)
    target_grid = patches.reshape(devices, block_count)
    slot_grid = row_of.reshape(devices, block_count)
    hits = target_grid == my_patch
    slot = jnp.max(jnp.where(hits, slot_grid, -1), axis=1)
    in_slot = slot[None, :] == jnp.arange(RS, dtype=jnp.int32)[:, None]
    one = jnp.where(in_slot[None], coeffs.T[:, None, :], 0.0)
    none = jnp.zeros_like(one)
    table = jnp.concatenate(
        [jnp.concatenate([one, none], axis=2), jnp.concatenate([none, one], axis=2)], axis=1
    ).reshape(channels * 2 * RS, 2 * devices).astype(jnp.bfloat16)
    places = jnp.arange(patch_rows, dtype=jnp.int32)
    edge = (margin + 7) // 8 * 8
    row_at = (places % RS) * row_count + places // RS + edge - margin
    across, down = band_tables(basis_across, basis_down, row_at[None, :], patch_rows + 2 * edge)
    received_rows = jnp.arange(row_count, dtype=jnp.int32)[None, :]
    row_in_patch = jnp.where(slot[:, None] >= 0, slot[:, None] * row_count + received_rows, -1)
    row_in_patch = row_in_patch.reshape(1, devices * row_count)
    kept, table, down, across, row_in_patch = lax.optimization_barrier((kept, table, down, across, row_in_patch))
    kept_in = lax.all_to_all(kept, BOTH, split_axis=0, concat_axis=0, tiled=True)
    at = jnp.stack([my_column, my_line]).astype(jnp.int32)
    down, across = (pltpu.with_memory_space_constraint(x, pltpu.HBM) for x in (down, across))
    inner, first, second = convolve_sum(margin, at, weighted_in, table, down, across)
    first, second = swap(first, "skyy", 0), swap(second, "skyy", 1)
    side = add_beside(at, inner, first, second)
    near, far = swap(side, "skyx", 0), swap(side, "skyx", 1)
    weight_sum = place_weights(row_in_patch, kept_in)
    coadd = finish(margin, at, inner, first, second, near, far)
    return (coadd, weight_sum)


def solution(mesh):
    placed = (P(BOTH, None, None), P(BOTH, None, None), P(), P(), P(), P(), P(), P(), P())
    return jax.shard_map(
        body,
        mesh=mesh,
        in_specs=placed,
        out_specs=(P("skyy", "skyx"), P("skyy", "skyx")),
        check_vma=False,
    )
```

```python
import functools

import jax
import jax.numpy as jnp
from jax import lax
from jax.experimental import pallas as pl
from jax.experimental.pallas import tpu as pltpu
from jax.sharding import PartitionSpec as P

RS = 4
LANES = 128
BOTH = ("skyx", "skyy")


def pack_kernel(planes, me, patch_of, valid, *refs):
    sources, refs = refs[:planes], refs[planes:]
    out, *rooms, packed, targets, usable, arrived, noted, sent = refs
    blocks = rooms[0].shape[0]
    chunks = arrived.shape[1]
    group = blocks // chunks

    def fetch(index, chunk):
        at = pl.ds(chunk * group, group)
        return pltpu.make_async_copy(sources[index].at[at], rooms[index].at[at], arrived.at[index, chunk])

    listed = targets.shape[0]
    devices_listed = listed // blocks
    some = pl.ds(pl.multiple_of(me[0] // devices_listed * listed, listed), listed)
    notes = [
        pltpu.make_async_copy(patch_of.at[some], targets, noted.at[0]),
        pltpu.make_async_copy(valid.at[some], usable, noted.at[1]),
    ]
    for note in notes:
        note.start()
    for chunk in range(chunks):
        for index in range(planes):
            fetch(index, chunk).start()
    packed[...] = jnp.zeros_like(packed)
    for note in notes:
        note.wait()
    first = me[0] % devices_listed * blocks
    for chunk in range(chunks):
        for index in range(planes):
            fetch(index, chunk).wait()
        for block in range(chunk * group, chunk * group + group):
            value = rooms[0][block]
            for room in rooms[1:]:
                value = value * room[block]
            place = targets[first + block]
            packed[place] = jnp.where(usable[first + block] != 0, value, jnp.zeros_like(value))
    pieces = sent.shape[0]
    share = packed.shape[0] // pieces
    copies = []
    for piece in range(pieces):
        at = pl.ds(piece * share, share)
        copies.append(pltpu.make_async_copy(packed.at[at], out.at[at], sent.at[piece]))
        copies[-1].start()
    for copy in copies:
        copy.wait()


def pack(devices, me, patch_of, valid, *planes):
    blocks, rows, width = planes[0].shape
    chunks, pieces = 4, 8
    return pl.pallas_call(
        functools.partial(pack_kernel, len(planes)),
        out_shape=jax.ShapeDtypeStruct((devices, rows, width), jnp.bfloat16),
        in_specs=[pl.BlockSpec(memory_space=pltpu.SMEM)] + [pl.BlockSpec(memory_space=pl.ANY)] * (2 + len(planes)),
        out_specs=pl.BlockSpec(memory_space=pl.ANY),
        scratch_shapes=[pltpu.VMEM((blocks, rows, width), jnp.bfloat16) for _ in planes]
        + [
            pltpu.VMEM((devices, rows, width), jnp.bfloat16),
            pltpu.SMEM((1024,), jnp.int32),
            pltpu.SMEM((1024,), jnp.int32),
            pltpu.SemaphoreType.DMA((len(planes), chunks)),
            pltpu.SemaphoreType.DMA((2,)),
            pltpu.SemaphoreType.DMA((pieces,)),
        ],
        cost_estimate=pl.CostEstimate(
            flops=devices * rows * width,
            bytes_accessed=2 * (len(planes) * blocks + devices) * rows * width,
            transcendentals=0,
        ),
        compiler_params=pltpu.CompilerParams(vmem_limit_bytes=63 << 20),
        name="pack",
    )(me, patch_of, valid, *planes)


def table_kernel(across_taps, down_taps, row_at, across, down):
    count, ext, places = down.shape
    lane = lax.broadcasted_iota(jnp.int32, (LANES, LANES), 1)
    line = lax.broadcasted_iota(jnp.int32, (LANES, LANES), 0)
    order = (lax.broadcasted_iota(jnp.int32, (LANES, places), 0) == row_at[...]).astype(jnp.bfloat16)
    for c in range(count):
        turned = jnp.broadcast_to(across_taps[c : c + 1, :], (LANES, LANES))
        turned = pltpu.roll(turned, 0, 1, stride=1, stride_axis=0)
        across[c, LANES:, :] = jnp.where(lane >= line, turned, 0.0).astype(jnp.bfloat16)
        across[c, :LANES, :] = jnp.where(lane < line, turned, 0.0).astype(jnp.bfloat16)
        turned = jnp.broadcast_to(down_taps[c : c + 1, :], (LANES, LANES))
        turned = pltpu.roll(turned, 0, 1, stride=1, stride_axis=0)[:ext].astype(jnp.bfloat16)
        down[c] = jnp.dot(turned, order, preferred_element_type=jnp.float32).astype(jnp.bfloat16)


def band_tables(basis_across, basis_down, row_at, ext):
    channels, taps = basis_across.shape
    places = row_at.shape[1]
    across_taps = jnp.pad(basis_across, ((0, 0), (0, LANES - taps)))
    down_taps = jnp.concatenate(
        [basis_down[:, :1], jnp.zeros((channels, LANES - taps), jnp.float32), basis_down[:, :0:-1]], axis=1
    )
    return pl.pallas_call(
        table_kernel,
        out_shape=(
            jax.ShapeDtypeStruct((channels, 2 * LANES, LANES), jnp.bfloat16),
            jax.ShapeDtypeStruct((channels, ext, places), jnp.bfloat16),
        ),
        in_specs=[pl.BlockSpec(memory_space=pltpu.VMEM)] * 3,
        out_specs=(pl.BlockSpec(memory_space=pltpu.VMEM),) * 2,
        compiler_params=pltpu.CompilerParams(vmem_limit_bytes=8 << 20),
        name="band_tables",
    )(across_taps, down_taps, row_at)


def coadd_kernel(
    margin, here, flux_far, choose, down_far, across_far, inner, first, second,
    flux, down, across, wide, channels, mixed, arrived,
):
    sources, rows, width = flux.shape
    count, ext, _ = down.shape
    pieces = width // LANES
    tiles = pieces + 1
    edge = first.shape[0]
    tall = inner.shape[0]
    chunks = arrived.shape[0] - 2
    share = sources // chunks
    copies = []
    for chunk in range(chunks):
        some = pl.ds(chunk * share, share)
        copies.append(pltpu.make_async_copy(flux_far.at[some], flux.at[some], arrived.at[chunk]))
    copies.append(pltpu.make_async_copy(down_far, down, arrived.at[chunks]))
    copies.append(pltpu.make_async_copy(across_far, across, arrived.at[chunks + 1]))
    for copy in copies:
        copy.start()
    for chunk in range(chunks):
        copies[chunk].wait()
        some = pl.ds(chunk * share, share)
        for piece in range(pieces):
            lanes = pl.ds(piece * LANES, LANES)
            block = flux[some, :, lanes].reshape(share * rows, LANES)
            wide[piece, pl.ds(chunk * share * rows, share * rows), :] = block.astype(jnp.float32)
    table = choose[...]
    for pair in range(rows // 2):
        halves = []
        for half in range(2):
            at = pl.ds(2 * pair + half, sources, stride=rows)
            row = [wide[piece, at, :].astype(jnp.bfloat16) for piece in range(pieces)]
            halves.append(jnp.concatenate(row, axis=1))
        summed = jnp.dot(table, jnp.concatenate(halves, axis=0), preferred_element_type=jnp.float32)
        channels[:, pair * 8 : pair * 8 + 8, :] = summed.reshape(count, 8, width)
    copies[chunks].wait()
    copies[chunks + 1].wait()
    zeros = jnp.zeros((ext, LANES), jnp.bfloat16)
    for c in range(count):
        mixed[c, :, :LANES] = zeros
        mixed[c, :, LANES + width :] = zeros
        mixed[c, :, LANES : LANES + width] = jnp.dot(
            down[c], channels[c].astype(jnp.bfloat16), preferred_element_type=jnp.float32
        ).astype(jnp.bfloat16)
    total = jnp.zeros((tiles * ext, LANES), jnp.float32)
    for c in range(count):
        windows = jnp.concatenate([mixed[c, :, LANES * t : LANES * t + 2 * LANES] for t in range(tiles)], axis=0)
        total = total + jnp.dot(windows, across[c], preferred_element_type=jnp.float32)
    whole = jnp.concatenate([total[t * ext : (t + 1) * ext] for t in range(tiles)], axis=1)
    whole = pltpu.roll(whole, tiles * LANES - margin, 1)
    inner[...] = whole[edge : edge + tall]
    top, bottom = whole[:edge], whole[edge + tall :]
    even = lax.rem(here[1], 2) == 0
    first[...] = jnp.where(even, bottom, top)
    second[...] = jnp.where(even, top, bottom)


def convolve_sum(margin, at, flux, choose, down, across):
    sources, rows, width = flux.shape
    count, ext, _ = down.shape
    tiles = width // LANES + 1
    tall = RS * rows
    edge = (ext - tall) // 2
    sizes = [(tall, tiles * LANES), (edge, tiles * LANES), (edge, tiles * LANES)]
    return pl.pallas_call(
        functools.partial(coadd_kernel, margin),
        out_shape=tuple(jax.ShapeDtypeStruct(size, jnp.float32) for size in sizes),
        in_specs=[
            pl.BlockSpec(memory_space=pltpu.SMEM),
            pl.BlockSpec(memory_space=pltpu.HBM),
            pl.BlockSpec(memory_space=pltpu.VMEM),
            pl.BlockSpec(memory_space=pltpu.HBM),
            pl.BlockSpec(memory_space=pltpu.HBM),
        ],
        out_specs=(pl.BlockSpec(memory_space=pltpu.VMEM),) * len(sizes),
        scratch_shapes=[
            pltpu.VMEM(flux.shape, jnp.bfloat16),
            pltpu.VMEM(down.shape, jnp.bfloat16),
            pltpu.VMEM(across.shape, jnp.bfloat16),
            pltpu.VMEM((width // LANES, sources * rows, LANES), jnp.float32),
            pltpu.VMEM((count, RS * rows, width), jnp.float32),
            pltpu.VMEM((count, ext, (tiles + 1) * LANES), jnp.bfloat16),
            pltpu.SemaphoreType.DMA((4 + 2,)),
        ],
        compiler_params=pltpu.CompilerParams(vmem_limit_bytes=20 << 20),
        cost_estimate=pl.CostEstimate(
            flops=2 * count * ext * tiles * LANES * 2 * LANES,
            bytes_accessed=2 * sources * rows * width + 4 * ext * tiles * LANES,
            transcendentals=0,
        ),
        name="convolve_sum",
    )(at, flux, choose, down, across)


def weight_kernel(row_in_patch, kept, out):
    sources, rows, width = kept.shape
    line = lax.broadcasted_iota(jnp.int32, (out.shape[0], sources * rows), 0)
    chosen = (line == row_in_patch[...]).astype(jnp.bfloat16)
    out[...] = jnp.dot(chosen, kept[...].reshape(sources * rows, width), preferred_element_type=jnp.float32)


def place_weights(row_in_patch, kept):
    sources, rows, width = kept.shape
    return pl.pallas_call(
        weight_kernel,
        out_shape=jax.ShapeDtypeStruct((RS * rows, width), jnp.float32),
        in_specs=[pl.BlockSpec(memory_space=pltpu.VMEM)] * 2,
        out_specs=pl.BlockSpec(memory_space=pltpu.VMEM),
        compiler_params=pltpu.CompilerParams(vmem_limit_bytes=8 << 20),
        cost_estimate=pl.CostEstimate(
            flops=2 * RS * rows * sources * rows * width,
            bytes_accessed=2 * sources * rows * width,
            transcendentals=0,
        ),
        name="place_weights",
    )(row_in_patch, kept)


def by_parity(place, first, second):
    even = lax.rem(place, 2) == 0
    return jnp.where(even, second, first), jnp.where(even, first, second)


def side_kernel(at, inner, first, second, out):
    tall, wide = inner.shape
    edge = first.shape[0]
    lanes = slice(wide - LANES, wide)
    above, below = by_parity(at[1], first[:, lanes], second[:, lanes])
    out[:edge, :] = inner[:edge, lanes] + above
    out[edge : tall - edge, :] = inner[edge : tall - edge, lanes]
    out[tall - edge :, :] = inner[tall - edge :, lanes] + below


def add_beside(at, inner, first, second):
    return pl.pallas_call(
        side_kernel,
        out_shape=jax.ShapeDtypeStruct((inner.shape[0], LANES), jnp.float32),
        in_specs=[pl.BlockSpec(memory_space=pltpu.SMEM)] + [pl.BlockSpec(memory_space=pltpu.VMEM)] * 3,
        out_specs=pl.BlockSpec(memory_space=pltpu.VMEM),
        compiler_params=pltpu.CompilerParams(vmem_limit_bytes=4 << 20),
        name="add_beside",
    )(at, inner, first, second)


def finish_kernel(margin, at, inner, first, second, near, far, out):
    tall, width = out.shape
    edge = first.shape[0]
    above, below = by_parity(at[1], first[:, :width], second[:, :width])
    out[:edge, :] = inner[:edge, :width] + above
    out[edge : tall - edge, :] = inner[edge : tall - edge, :width]
    out[tall - edge :, :] = inner[tall - edge :, :width] + below
    lane = lax.broadcasted_iota(jnp.int32, (1, LANES), 1)
    left, right = by_parity(at[0], near[...], far[...])
    out[:, :LANES] += jnp.where(lane < margin, left, 0.0)
    out[:, width - LANES :] += jnp.where(lane >= LANES - margin, right, 0.0)


def finish(margin, at, inner, first, second, near, far):
    tall, wide = inner.shape
    return pl.pallas_call(
        functools.partial(finish_kernel, margin),
        out_shape=jax.ShapeDtypeStruct((tall, wide - LANES), jnp.float32),
        in_specs=[pl.BlockSpec(memory_space=pltpu.SMEM)] + [pl.BlockSpec(memory_space=pltpu.VMEM)] * 5,
        out_specs=pl.BlockSpec(memory_space=pltpu.VMEM),
        compiler_params=pltpu.CompilerParams(vmem_limit_bytes=4 << 20),
        name="finish",
    )(at, inner, first, second, near, far)


def swap(value, axis, first):
    pairs = [(i, i + 1) for i in range(first, lax.axis_size(axis) - 1, 2)]
    return lax.ppermute(value, axis, pairs + [(j, i) for i, j in pairs])


def body(
    image, inverse_var, patch_of, row_of, valid, coef_index, coef_table, basis_across, basis_down
):
    devices = lax.axis_size("skyx") * lax.axis_size("skyy")
    block_count, row_count, block_width = image.shape
    channels = basis_across.shape[0]
    margin = (basis_across.shape[1] - 1) // 2
    patch_rows = RS * row_count
    columns, lines = lax.axis_size("skyx"), lax.axis_size("skyy")
    my_column, my_line = lax.axis_index("skyx"), lax.axis_index("skyy")
    my_patch = my_column * lines + my_line
    patches = patch_of[:, 0]
    me = my_patch.astype(jnp.int32).reshape(1)

    weighted = pack(devices, me, patches, valid, inverse_var, image)
    weighted_in = lax.all_to_all(weighted, BOTH, split_axis=0, concat_axis=0, tiled=True)
    kept = pack(devices, me, patches, valid, inverse_var)

    choose = (
        coef_index[:, None] == jnp.arange(coef_table.shape[0], dtype=jnp.int32)[None, :]
    ).astype(jnp.float32)
    coeffs = jnp.dot(choose, coef_table, precision=lax.Precision.HIGHEST)
    target_grid = patches.reshape(devices, block_count)
    slot_grid = row_of.reshape(devices, block_count)
    hits = target_grid == my_patch
    slot = jnp.max(jnp.where(hits, slot_grid, -1), axis=1)
    in_slot = slot[None, :] == jnp.arange(RS, dtype=jnp.int32)[:, None]
    one = jnp.where(in_slot[None], coeffs.T[:, None, :], 0.0)
    none = jnp.zeros_like(one)
    table = jnp.concatenate(
        [jnp.concatenate([one, none], axis=2), jnp.concatenate([none, one], axis=2)], axis=1
    ).reshape(channels * 2 * RS, 2 * devices).astype(jnp.bfloat16)
    places = jnp.arange(patch_rows, dtype=jnp.int32)
    edge = (margin + 7) // 8 * 8
    row_at = (places % RS) * row_count + places // RS + edge - margin
    across, down = band_tables(basis_across, basis_down, row_at[None, :], patch_rows + 2 * edge)
    received_rows = jnp.arange(row_count, dtype=jnp.int32)[None, :]
    row_in_patch = jnp.where(slot[:, None] >= 0, slot[:, None] * row_count + received_rows, -1)
    row_in_patch = row_in_patch.reshape(1, devices * row_count)
    kept, table, down, across, row_in_patch = lax.optimization_barrier((kept, table, down, across, row_in_patch))
    kept_in = lax.all_to_all(kept, BOTH, split_axis=0, concat_axis=0, tiled=True)
    at = jnp.stack([my_column, my_line]).astype(jnp.int32)
    down, across = (pltpu.with_memory_space_constraint(x, pltpu.HBM) for x in (down, across))
    inner, first, second = convolve_sum(margin, at, weighted_in, table, down, across)
    first, second = swap(first, "skyy", 0), swap(second, "skyy", 1)
    side = add_beside(at, inner, first, second)
    near, far = swap(side, "skyx", 0), swap(side, "skyx", 1)
    weight_sum = place_weights(row_in_patch, kept_in)
    coadd = finish(margin, at, inner, first, second, near, far)
    return (coadd, weight_sum)


def solution(mesh):
    placed = (P(BOTH, None, None), P(BOTH, None, None), P(), P(), P(), P(), P(), P(), P())
    return jax.shard_map(
        body,
        mesh=mesh,
        in_specs=placed,
        out_specs=(P("skyy", "skyx"), P("skyy", "skyx")),
        check_vma=False,
    )
```

```python
import functools

import jax
import jax.numpy as jnp
from jax import lax
from jax.experimental import pallas as pl
from jax.experimental.pallas import tpu as pltpu
from jax.sharding import PartitionSpec as P

RS = 4
LANES = 128
BOTH = ("skyx", "skyy")


def pack_kernel(planes, me, patch_of, valid, *refs):
    sources, refs = refs[:planes], refs[planes:]
    out, *rooms, packed, targets, usable, arrived, noted, sent = refs
    blocks = rooms[0].shape[0]
    chunks = arrived.shape[1]
    group = blocks // chunks

    def fetch(index, chunk):
        at = pl.ds(chunk * group, group)
        return pltpu.make_async_copy(sources[index].at[at], rooms[index].at[at], arrived.at[index, chunk])

    listed = targets.shape[0]
    devices_listed = listed // blocks
    some = pl.ds(pl.multiple_of(me[0] // devices_listed * listed, listed), listed)
    notes = [
        pltpu.make_async_copy(patch_of.at[some], targets, noted.at[0]),
        pltpu.make_async_copy(valid.at[some], usable, noted.at[1]),
    ]
    for note in notes:
        note.start()
    for chunk in range(chunks):
        for index in range(planes):
            fetch(index, chunk).start()
    unsent = packed.shape[0] - 1
    packed[...] = jnp.zeros_like(packed)
    for note in notes:
        note.wait()
    first = me[0] % devices_listed * blocks
    for chunk in range(chunks):
        for index in range(planes):
            fetch(index, chunk).wait()
        for block in range(chunk * group, chunk * group + group):
            value = rooms[0][block]
            for room in rooms[1:]:
                value = value * room[block]
            place = jnp.where(usable[first + block] != 0, targets[first + block], unsent)
            packed[place] = value
    pieces = sent.shape[0]
    share = unsent // pieces
    copies = []
    for piece in range(pieces):
        at = pl.ds(piece * share, share)
        copies.append(pltpu.make_async_copy(packed.at[at], out.at[at], sent.at[piece]))
        copies[-1].start()
    for copy in copies:
        copy.wait()


def pack(devices, me, patch_of, valid, *planes):
    blocks, rows, width = planes[0].shape
    chunks, pieces = 2, 2
    return pl.pallas_call(
        functools.partial(pack_kernel, len(planes)),
        out_shape=jax.ShapeDtypeStruct((devices, rows, width), jnp.bfloat16),
        in_specs=[pl.BlockSpec(memory_space=pltpu.SMEM)] + [pl.BlockSpec(memory_space=pl.ANY)] * (2 + len(planes)),
        out_specs=pl.BlockSpec(memory_space=pl.ANY),
        scratch_shapes=[pltpu.VMEM((blocks, rows, width), jnp.bfloat16) for _ in planes]
        + [
            pltpu.VMEM((devices + 1, rows, width), jnp.bfloat16),
            pltpu.SMEM((1024,), jnp.int32),
            pltpu.SMEM((1024,), jnp.int32),
            pltpu.SemaphoreType.DMA((len(planes), chunks)),
            pltpu.SemaphoreType.DMA((2,)),
            pltpu.SemaphoreType.DMA((pieces,)),
        ],
        cost_estimate=pl.CostEstimate(
            flops=devices * rows * width,
            bytes_accessed=2 * (len(planes) * blocks + devices) * rows * width,
            transcendentals=0,
        ),
        compiler_params=pltpu.CompilerParams(vmem_limit_bytes=63 << 20),
        name="pack",
    )(me, patch_of, valid, *planes)


def table_kernel(across_taps, down_taps, row_at, across, down):
    count, ext, places = down.shape
    lane = lax.broadcasted_iota(jnp.int32, (LANES, LANES), 1)
    line = lax.broadcasted_iota(jnp.int32, (LANES, LANES), 0)
    order = (lax.broadcasted_iota(jnp.int32, (LANES, places), 0) == row_at[...]).astype(jnp.bfloat16)
    for c in range(count):
        turned = jnp.broadcast_to(across_taps[c : c + 1, :], (LANES, LANES))
        turned = pltpu.roll(turned, 0, 1, stride=1, stride_axis=0)
        across[c, LANES:, :] = jnp.where(lane >= line, turned, 0.0).astype(jnp.bfloat16)
        across[c, :LANES, :] = jnp.where(lane < line, turned, 0.0).astype(jnp.bfloat16)
        turned = jnp.broadcast_to(down_taps[c : c + 1, :], (LANES, LANES))
        turned = pltpu.roll(turned, 0, 1, stride=1, stride_axis=0)[:ext].astype(jnp.bfloat16)
        down[c] = jnp.dot(turned, order, preferred_element_type=jnp.float32).astype(jnp.bfloat16)


def band_tables(basis_across, basis_down, row_at, ext):
    channels, taps = basis_across.shape
    places = row_at.shape[1]
    across_taps = jnp.pad(basis_across, ((0, 0), (0, LANES - taps)))
    down_taps = jnp.concatenate(
        [basis_down[:, :1], jnp.zeros((channels, LANES - taps), jnp.float32), basis_down[:, :0:-1]], axis=1
    )
    return pl.pallas_call(
        table_kernel,
        out_shape=(
            jax.ShapeDtypeStruct((channels, 2 * LANES, LANES), jnp.bfloat16),
            jax.ShapeDtypeStruct((channels, ext, places), jnp.bfloat16),
        ),
        in_specs=[pl.BlockSpec(memory_space=pltpu.VMEM)] * 3,
        out_specs=(pl.BlockSpec(memory_space=pltpu.VMEM),) * 2,
        compiler_params=pltpu.CompilerParams(vmem_limit_bytes=8 << 20),
        name="band_tables",
    )(across_taps, down_taps, row_at)


def coadd_kernel(
    margin, here, flux_far, choose, down_far, across_far, inner, first, second,
    flux, down, across, wide, channels, mixed, arrived,
):
    sources, rows, width = flux.shape
    count, ext, _ = down.shape
    pieces = width // LANES
    tiles = pieces + 1
    edge = first.shape[0]
    tall = inner.shape[0]
    chunks = arrived.shape[0] - 2
    share = sources // chunks
    copies = []
    for chunk in range(chunks):
        some = pl.ds(chunk * share, share)
        copies.append(pltpu.make_async_copy(flux_far.at[some], flux.at[some], arrived.at[chunk]))
    copies.append(pltpu.make_async_copy(down_far, down, arrived.at[chunks]))
    copies.append(pltpu.make_async_copy(across_far, across, arrived.at[chunks + 1]))
    for copy in copies:
        copy.start()
    for chunk in range(chunks):
        copies[chunk].wait()
        some = pl.ds(chunk * share, share)
        for piece in range(pieces):
            lanes = pl.ds(piece * LANES, LANES)
            block = flux[some, :, lanes].reshape(share * rows, LANES)
            wide[piece, pl.ds(chunk * share * rows, share * rows), :] = block.astype(jnp.float32)
    table = choose[...]
    for pair in range(rows // 2):
        halves = []
        for half in range(2):
            at = pl.ds(2 * pair + half, sources, stride=rows)
            row = [wide[piece, at, :].astype(jnp.bfloat16) for piece in range(pieces)]
            halves.append(jnp.concatenate(row, axis=1))
        summed = jnp.dot(table, jnp.concatenate(halves, axis=0), preferred_element_type=jnp.float32)
        channels[:, pair * 8 : pair * 8 + 8, :] = summed.reshape(count, 8, width)
    copies[chunks].wait()
    copies[chunks + 1].wait()
    zeros = jnp.zeros((ext, LANES), jnp.bfloat16)
    for c in range(count):
        mixed[c, :, :LANES] = zeros
        mixed[c, :, LANES + width :] = zeros
        mixed[c, :, LANES : LANES + width] = jnp.dot(
            down[c], channels[c].astype(jnp.bfloat16), preferred_element_type=jnp.float32
        ).astype(jnp.bfloat16)
    total = jnp.zeros((tiles * ext, LANES), jnp.float32)
    for c in range(count):
        windows = jnp.concatenate([mixed[c, :, LANES * t : LANES * t + 2 * LANES] for t in range(tiles)], axis=0)
        total = total + jnp.dot(windows, across[c], preferred_element_type=jnp.float32)
    whole = jnp.concatenate([total[t * ext : (t + 1) * ext] for t in range(tiles)], axis=1)
    whole = pltpu.roll(whole, tiles * LANES - margin, 1)
    inner[...] = whole[edge : edge + tall]
    top, bottom = whole[:edge], whole[edge + tall :]
    even = lax.rem(here[1], 2) == 0
    first[...] = jnp.where(even, bottom, top).astype(first.dtype)
    second[...] = jnp.where(even, top, bottom).astype(second.dtype)


def convolve_sum(margin, at, flux, choose, down, across):
    sources, rows, width = flux.shape
    count, ext, _ = down.shape
    tiles = width // LANES + 1
    tall = RS * rows
    edge = (ext - tall) // 2
    sizes = [(tall, tiles * LANES), (edge, tiles * LANES), (edge, tiles * LANES)]
    types = (jnp.float32, jnp.bfloat16, jnp.bfloat16)
    return pl.pallas_call(
        functools.partial(coadd_kernel, margin),
        out_shape=tuple(jax.ShapeDtypeStruct(*array) for array in zip(sizes, types)),
        in_specs=[
            pl.BlockSpec(memory_space=pltpu.SMEM),
            pl.BlockSpec(memory_space=pltpu.HBM),
            pl.BlockSpec(memory_space=pltpu.VMEM),
            pl.BlockSpec(memory_space=pltpu.HBM),
            pl.BlockSpec(memory_space=pltpu.HBM),
        ],
        out_specs=(pl.BlockSpec(memory_space=pltpu.VMEM),) * len(sizes),
        scratch_shapes=[
            pltpu.VMEM(flux.shape, jnp.bfloat16),
            pltpu.VMEM(down.shape, jnp.bfloat16),
            pltpu.VMEM(across.shape, jnp.bfloat16),
            pltpu.VMEM((width // LANES, sources * rows, LANES), jnp.float32),
            pltpu.VMEM((count, RS * rows, width), jnp.float32),
            pltpu.VMEM((count, ext, (tiles + 1) * LANES), jnp.bfloat16),
            pltpu.SemaphoreType.DMA((4 + 2,)),
        ],
        compiler_params=pltpu.CompilerParams(vmem_limit_bytes=20 << 20),
        cost_estimate=pl.CostEstimate(
            flops=2 * count * ext * tiles * LANES * 2 * LANES,
            bytes_accessed=2 * sources * rows * width + 4 * ext * tiles * LANES,
            transcendentals=0,
        ),
        name="convolve_sum",
    )(at, flux, choose, down, across)


def weight_kernel(row_in_patch, kept, out):
    sources, rows, width = kept.shape
    line = lax.broadcasted_iota(jnp.int32, (out.shape[0], sources * rows), 0)
    chosen = (line == row_in_patch[...]).astype(jnp.bfloat16)
    out[...] = jnp.dot(chosen, kept[...].reshape(sources * rows, width), preferred_element_type=jnp.float32)


def place_weights(row_in_patch, kept):
    sources, rows, width = kept.shape
    return pl.pallas_call(
        weight_kernel,
        out_shape=jax.ShapeDtypeStruct((RS * rows, width), jnp.float32),
        in_specs=[pl.BlockSpec(memory_space=pltpu.VMEM)] * 2,
        out_specs=pl.BlockSpec(memory_space=pltpu.VMEM),
        compiler_params=pltpu.CompilerParams(vmem_limit_bytes=8 << 20),
        cost_estimate=pl.CostEstimate(
            flops=2 * RS * rows * sources * rows * width,
            bytes_accessed=2 * sources * rows * width,
            transcendentals=0,
        ),
        name="place_weights",
    )(row_in_patch, kept)


def by_parity(place, first, second):
    even = lax.rem(place, 2) == 0
    first, second = first.astype(jnp.float32), second.astype(jnp.float32)
    return jnp.where(even, second, first), jnp.where(even, first, second)


def side_kernel(at, inner, first, second, out):
    tall, wide = inner.shape
    edge = first.shape[0]
    lanes = slice(wide - LANES, wide)
    above, below = by_parity(at[1], first[:, lanes], second[:, lanes])
    out[:edge, :] = (inner[:edge, lanes] + above).astype(out.dtype)
    out[edge : tall - edge, :] = inner[edge : tall - edge, lanes].astype(out.dtype)
    out[tall - edge :, :] = (inner[tall - edge :, lanes] + below).astype(out.dtype)


def add_beside(at, inner, first, second):
    return pl.pallas_call(
        side_kernel,
        out_shape=jax.ShapeDtypeStruct((inner.shape[0], LANES), jnp.bfloat16),
        in_specs=[pl.BlockSpec(memory_space=pltpu.SMEM)] + [pl.BlockSpec(memory_space=pltpu.VMEM)] * 3,
        out_specs=pl.BlockSpec(memory_space=pltpu.VMEM),
        compiler_params=pltpu.CompilerParams(vmem_limit_bytes=4 << 20),
        name="add_beside",
    )(at, inner, first, second)


def finish_kernel(margin, at, inner, first, second, near, far, out):
    tall, width = out.shape
    edge = first.shape[0]
    above, below = by_parity(at[1], first[:, :width], second[:, :width])
    out[:edge, :] = inner[:edge, :width] + above
    out[edge : tall - edge, :] = inner[edge : tall - edge, :width]
    out[tall - edge :, :] = inner[tall - edge :, :width] + below
    lane = lax.broadcasted_iota(jnp.int32, (1, LANES), 1)
    left, right = by_parity(at[0], near[...], far[...])
    out[:, :LANES] += jnp.where(lane < margin, left, 0.0)
    out[:, width - LANES :] += jnp.where(lane >= LANES - margin, right, 0.0)


def finish(margin, at, inner, first, second, near, far):
    tall, wide = inner.shape
    return pl.pallas_call(
        functools.partial(finish_kernel, margin),
        out_shape=jax.ShapeDtypeStruct((tall, wide - LANES), jnp.float32),
        in_specs=[pl.BlockSpec(memory_space=pltpu.SMEM)] + [pl.BlockSpec(memory_space=pltpu.VMEM)] * 5,
        out_specs=pl.BlockSpec(memory_space=pltpu.VMEM),
        compiler_params=pltpu.CompilerParams(vmem_limit_bytes=4 << 20),
        name="finish",
    )(at, inner, first, second, near, far)


def swap(value, axis, first):
    pairs = [(i, i + 1) for i in range(first, lax.axis_size(axis) - 1, 2)]
    return lax.ppermute(value, axis, pairs + [(j, i) for i, j in pairs])


def body(
    image, inverse_var, patch_of, row_of, valid, coef_index, coef_table, basis_across, basis_down
):
    devices = lax.axis_size("skyx") * lax.axis_size("skyy")
    block_count, row_count, block_width = image.shape
    channels = basis_across.shape[0]
    margin = (basis_across.shape[1] - 1) // 2
    patch_rows = RS * row_count
    columns, lines = lax.axis_size("skyx"), lax.axis_size("skyy")
    my_column, my_line = lax.axis_index("skyx"), lax.axis_index("skyy")
    my_patch = my_column * lines + my_line
    patches = patch_of[:, 0]
    me = my_patch.astype(jnp.int32).reshape(1)

    weighted = pack(devices, me, patches, valid, inverse_var, image)
    weighted_in = lax.all_to_all(weighted, BOTH, split_axis=0, concat_axis=0, tiled=True)
    kept = pack(devices, me, patches, valid, inverse_var)

    choose = (
        coef_index[:, None] == jnp.arange(coef_table.shape[0], dtype=jnp.int32)[None, :]
    ).astype(jnp.float32)
    coeffs = jnp.dot(choose, coef_table, precision=lax.Precision.HIGHEST)
    target_grid = patches.reshape(devices, block_count)
    slot_grid = row_of.reshape(devices, block_count)
    hits = target_grid == my_patch
    slot = jnp.max(jnp.where(hits, slot_grid, -1), axis=1)
    in_slot = slot[None, :] == jnp.arange(RS, dtype=jnp.int32)[:, None]
    one = jnp.where(in_slot[None], coeffs.T[:, None, :], 0.0)
    none = jnp.zeros_like(one)
    table = jnp.concatenate(
        [jnp.concatenate([one, none], axis=2), jnp.concatenate([none, one], axis=2)], axis=1
    ).reshape(channels * 2 * RS, 2 * devices).astype(jnp.bfloat16)
    places = jnp.arange(patch_rows, dtype=jnp.int32)
    edge = (margin + 7) // 8 * 8
    row_at = (places % RS) * row_count + places // RS + edge - margin
    across, down = band_tables(basis_across, basis_down, row_at[None, :], patch_rows + 2 * edge)
    received_rows = jnp.arange(row_count, dtype=jnp.int32)[None, :]
    row_in_patch = jnp.where(slot[:, None] >= 0, slot[:, None] * row_count + received_rows, -1)
    row_in_patch = row_in_patch.reshape(1, devices * row_count)
    kept, table, down, across, row_in_patch = lax.optimization_barrier((kept, table, down, across, row_in_patch))
    kept_in = lax.all_to_all(kept, BOTH, split_axis=0, concat_axis=0, tiled=True)
    at = jnp.stack([my_column, my_line]).astype(jnp.int32)
    down, across = (pltpu.with_memory_space_constraint(x, pltpu.HBM) for x in (down, across))
    inner, first, second = convolve_sum(margin, at, weighted_in, table, down, across)
    first, second = swap(first, "skyy", 0), swap(second, "skyy", 1)
    side = add_beside(at, inner, first, second)
    near, far = swap(side, "skyx", 0), swap(side, "skyx", 1)
    weight_sum = place_weights(row_in_patch, kept_in)
    coadd = finish(margin, at, inner, first, second, near, far)
    return (coadd, weight_sum)


def solution(mesh):
    placed = (P(BOTH, None, None), P(BOTH, None, None), P(), P(), P(), P(), P(), P(), P())
    return jax.shard_map(
        body,
        mesh=mesh,
        in_specs=placed,
        out_specs=(P("skyy", "skyx"), P("skyy", "skyx")),
        check_vma=False,
    )
```

```python
import functools

import jax
import jax.numpy as jnp
from jax import lax
from jax.experimental import pallas as pl
from jax.experimental.pallas import tpu as pltpu
from jax.sharding import PartitionSpec as P

RS = 4
LANES = 128
BOTH = ("skyx", "skyy")


def pack_kernel(planes, patch_of, valid, *refs):
    me = lax.axis_index(BOTH)
    sources, refs = refs[:planes], refs[planes:]
    out, *rooms, packed, targets, usable, arrived, noted, sent = refs
    blocks = rooms[0].shape[0]
    chunks = arrived.shape[1]
    group = blocks // chunks

    def fetch(index, chunk):
        at = pl.ds(chunk * group, group)
        return pltpu.make_async_copy(sources[index].at[at], rooms[index].at[at], arrived.at[index, chunk])

    listed = targets.shape[0]
    devices_listed = listed // blocks
    some = pl.ds(pl.multiple_of(me // devices_listed * listed, listed), listed)
    notes = [
        pltpu.make_async_copy(patch_of.at[some], targets, noted.at[0]),
        pltpu.make_async_copy(valid.at[some], usable, noted.at[1]),
    ]
    for note in notes:
        note.start()
    for chunk in range(chunks):
        for index in range(planes):
            fetch(index, chunk).start()
    unsent = packed.shape[0] - 1
    packed[...] = jnp.zeros_like(packed)
    for note in notes:
        note.wait()
    first = me % devices_listed * blocks
    for chunk in range(chunks):
        for index in range(planes):
            fetch(index, chunk).wait()
        for block in range(chunk * group, chunk * group + group):
            value = rooms[0][block]
            for room in rooms[1:]:
                value = value * room[block]
            place = jnp.where(usable[first + block] != 0, targets[first + block], unsent)
            packed[place] = value
    pieces = sent.shape[0]
    share = unsent // pieces
    copies = []
    for piece in range(pieces):
        at = pl.ds(piece * share, share)
        copies.append(pltpu.make_async_copy(packed.at[at], out.at[at], sent.at[piece]))
        copies[-1].start()
    for copy in copies:
        copy.wait()


def pack(devices, patch_of, valid, *planes):
    blocks, rows, width = planes[0].shape
    chunks, pieces = 2, 2
    return pl.pallas_call(
        functools.partial(pack_kernel, len(planes)),
        out_shape=jax.ShapeDtypeStruct((devices, rows, width), jnp.bfloat16),
        in_specs=[pl.BlockSpec(memory_space=pl.ANY)] * (2 + len(planes)),
        out_specs=pl.BlockSpec(memory_space=pl.ANY),
        scratch_shapes=[pltpu.VMEM((blocks, rows, width), jnp.bfloat16) for _ in planes]
        + [
            pltpu.VMEM((devices + 1, rows, width), jnp.bfloat16),
            pltpu.SMEM((1024,), jnp.int32),
            pltpu.SMEM((1024,), jnp.int32),
            pltpu.SemaphoreType.DMA((len(planes), chunks)),
            pltpu.SemaphoreType.DMA((2,)),
            pltpu.SemaphoreType.DMA((pieces,)),
        ],
        cost_estimate=pl.CostEstimate(
            flops=devices * rows * width,
            bytes_accessed=2 * (len(planes) * blocks + devices) * rows * width,
            transcendentals=0,
        ),
        compiler_params=pltpu.CompilerParams(vmem_limit_bytes=63 << 20),
        name="pack",
    )(patch_of, valid, *planes)


def table_kernel(across_taps, down_taps, row_at, across, down):
    count, ext, places = down.shape
    lane = lax.broadcasted_iota(jnp.int32, (LANES, LANES), 1)
    line = lax.broadcasted_iota(jnp.int32, (LANES, LANES), 0)
    order = (lax.broadcasted_iota(jnp.int32, (LANES, places), 0) == row_at[...]).astype(jnp.bfloat16)
    for c in range(count):
        turned = jnp.broadcast_to(across_taps[c : c + 1, :], (LANES, LANES))
        turned = pltpu.roll(turned, 0, 1, stride=1, stride_axis=0)
        across[c, LANES:, :] = jnp.where(lane >= line, turned, 0.0).astype(jnp.bfloat16)
        across[c, :LANES, :] = jnp.where(lane < line, turned, 0.0).astype(jnp.bfloat16)
        turned = jnp.broadcast_to(down_taps[c : c + 1, :], (LANES, LANES))
        turned = pltpu.roll(turned, 0, 1, stride=1, stride_axis=0)[:ext].astype(jnp.bfloat16)
        down[c] = jnp.dot(turned, order, preferred_element_type=jnp.float32).astype(jnp.bfloat16)


def band_tables(basis_across, basis_down, row_at, ext):
    channels, taps = basis_across.shape
    places = row_at.shape[1]
    across_taps = jnp.pad(basis_across, ((0, 0), (0, LANES - taps)))
    down_taps = jnp.concatenate(
        [basis_down[:, :1], jnp.zeros((channels, LANES - taps), jnp.float32), basis_down[:, :0:-1]], axis=1
    )
    return pl.pallas_call(
        table_kernel,
        out_shape=(
            jax.ShapeDtypeStruct((channels, 2 * LANES, LANES), jnp.bfloat16),
            jax.ShapeDtypeStruct((channels, ext, places), jnp.bfloat16),
        ),
        in_specs=[pl.BlockSpec(memory_space=pltpu.VMEM)] * 3,
        out_specs=(pl.BlockSpec(memory_space=pltpu.VMEM),) * 2,
        compiler_params=pltpu.CompilerParams(vmem_limit_bytes=8 << 20),
        name="band_tables",
    )(across_taps, down_taps, row_at)


def coadd_kernel(
    margin, flux_far, choose, down_far, across_far, inner, first, second,
    flux, down, across, wide, channels, mixed, arrived,
):
    sources, rows, width = flux.shape
    count, ext, _ = down.shape
    pieces = width // LANES
    tiles = pieces + 1
    edge = first.shape[0]
    tall = inner.shape[0]
    chunks = arrived.shape[0] - 2
    share = sources // chunks
    copies = []
    for chunk in range(chunks):
        some = pl.ds(chunk * share, share)
        copies.append(pltpu.make_async_copy(flux_far.at[some], flux.at[some], arrived.at[chunk]))
    copies.append(pltpu.make_async_copy(down_far, down, arrived.at[chunks]))
    copies.append(pltpu.make_async_copy(across_far, across, arrived.at[chunks + 1]))
    for copy in copies:
        copy.start()
    for chunk in range(chunks):
        copies[chunk].wait()
        some = pl.ds(chunk * share, share)
        for piece in range(pieces):
            lanes = pl.ds(piece * LANES, LANES)
            block = flux[some, :, lanes].reshape(share * rows, LANES)
            wide[piece, pl.ds(chunk * share * rows, share * rows), :] = block.astype(jnp.float32)
    table = choose[...]
    for pair in range(rows // 2):
        halves = []
        for half in range(2):
            at = pl.ds(2 * pair + half, sources, stride=rows)
            row = [wide[piece, at, :].astype(jnp.bfloat16) for piece in range(pieces)]
            halves.append(jnp.concatenate(row, axis=1))
        summed = jnp.dot(table, jnp.concatenate(halves, axis=0), preferred_element_type=jnp.float32)
        channels[:, pair * 8 : pair * 8 + 8, :] = summed.reshape(count, 8, width)
    copies[chunks].wait()
    copies[chunks + 1].wait()
    zeros = jnp.zeros((ext, LANES), jnp.bfloat16)
    for c in range(count):
        mixed[c, :, :LANES] = zeros
        mixed[c, :, LANES + width :] = zeros
        mixed[c, :, LANES : LANES + width] = jnp.dot(
            down[c], channels[c].astype(jnp.bfloat16), preferred_element_type=jnp.float32
        ).astype(jnp.bfloat16)
    total = jnp.zeros((tiles * ext, LANES), jnp.float32)
    for c in range(count):
        windows = jnp.concatenate([mixed[c, :, LANES * t : LANES * t + 2 * LANES] for t in range(tiles)], axis=0)
        total = total + jnp.dot(windows, across[c], preferred_element_type=jnp.float32)
    whole = jnp.concatenate([total[t * ext : (t + 1) * ext] for t in range(tiles)], axis=1)
    whole = pltpu.roll(whole, tiles * LANES - margin, 1)
    inner[...] = whole[edge : edge + tall]
    top, bottom = whole[:edge], whole[edge + tall :]
    even = lax.rem(lax.axis_index("skyy"), 2) == 0
    first[...] = jnp.where(even, bottom, top).astype(first.dtype)
    second[...] = jnp.where(even, top, bottom).astype(second.dtype)


def convolve_sum(margin, flux, choose, down, across):
    sources, rows, width = flux.shape
    count, ext, _ = down.shape
    tiles = width // LANES + 1
    tall = RS * rows
    edge = (ext - tall) // 2
    sizes = [(tall, tiles * LANES), (edge, tiles * LANES), (edge, tiles * LANES)]
    types = (jnp.float32, jnp.bfloat16, jnp.bfloat16)
    return pl.pallas_call(
        functools.partial(coadd_kernel, margin),
        out_shape=tuple(jax.ShapeDtypeStruct(*array) for array in zip(sizes, types)),
        in_specs=[
            pl.BlockSpec(memory_space=pltpu.HBM),
            pl.BlockSpec(memory_space=pltpu.VMEM),
            pl.BlockSpec(memory_space=pltpu.HBM),
            pl.BlockSpec(memory_space=pltpu.HBM),
        ],
        out_specs=(pl.BlockSpec(memory_space=pltpu.VMEM),) * len(sizes),
        scratch_shapes=[
            pltpu.VMEM(flux.shape, jnp.bfloat16),
            pltpu.VMEM(down.shape, jnp.bfloat16),
            pltpu.VMEM(across.shape, jnp.bfloat16),
            pltpu.VMEM((width // LANES, sources * rows, LANES), jnp.float32),
            pltpu.VMEM((count, RS * rows, width), jnp.float32),
            pltpu.VMEM((count, ext, (tiles + 1) * LANES), jnp.bfloat16),
            pltpu.SemaphoreType.DMA((4 + 2,)),
        ],
        compiler_params=pltpu.CompilerParams(vmem_limit_bytes=20 << 20),
        cost_estimate=pl.CostEstimate(
            flops=2 * count * ext * tiles * LANES * 2 * LANES,
            bytes_accessed=2 * sources * rows * width + 4 * ext * tiles * LANES,
            transcendentals=0,
        ),
        name="convolve_sum",
    )(flux, choose, down, across)


def weight_kernel(row_in_patch, kept, out):
    sources, rows, width = kept.shape
    line = lax.broadcasted_iota(jnp.int32, (out.shape[0], sources * rows), 0)
    chosen = (line == row_in_patch[...]).astype(jnp.bfloat16)
    out[...] = jnp.dot(chosen, kept[...].reshape(sources * rows, width), preferred_element_type=jnp.float32)


def place_weights(row_in_patch, kept):
    sources, rows, width = kept.shape
    return pl.pallas_call(
        weight_kernel,
        out_shape=jax.ShapeDtypeStruct((RS * rows, width), jnp.float32),
        in_specs=[pl.BlockSpec(memory_space=pltpu.VMEM)] * 2,
        out_specs=pl.BlockSpec(memory_space=pltpu.VMEM),
        compiler_params=pltpu.CompilerParams(vmem_limit_bytes=8 << 20),
        cost_estimate=pl.CostEstimate(
            flops=2 * RS * rows * sources * rows * width,
            bytes_accessed=2 * sources * rows * width,
            transcendentals=0,
        ),
        name="place_weights",
    )(row_in_patch, kept)


def by_parity(axis, first, second):
    even = lax.rem(lax.axis_index(axis), 2) == 0
    first, second = first.astype(jnp.float32), second.astype(jnp.float32)
    return jnp.where(even, second, first), jnp.where(even, first, second)


def side_kernel(inner, first, second, out):
    tall, wide = inner.shape
    edge = first.shape[0]
    lanes = slice(wide - LANES, wide)
    above, below = by_parity("skyy", first[:, lanes], second[:, lanes])
    out[:edge, :] = (inner[:edge, lanes] + above).astype(out.dtype)
    out[edge : tall - edge, :] = inner[edge : tall - edge, lanes].astype(out.dtype)
    out[tall - edge :, :] = (inner[tall - edge :, lanes] + below).astype(out.dtype)


def add_beside(inner, first, second):
    return pl.pallas_call(
        side_kernel,
        out_shape=jax.ShapeDtypeStruct((inner.shape[0], LANES), jnp.bfloat16),
        in_specs=[pl.BlockSpec(memory_space=pltpu.VMEM)] * 3,
        out_specs=pl.BlockSpec(memory_space=pltpu.VMEM),
        compiler_params=pltpu.CompilerParams(vmem_limit_bytes=4 << 20),
        name="add_beside",
    )(inner, first, second)


def finish_kernel(margin, inner, first, second, near, far, out):
    tall, width = out.shape
    edge = first.shape[0]
    above, below = by_parity("skyy", first[:, :width], second[:, :width])
    out[:edge, :] = inner[:edge, :width] + above
    out[edge : tall - edge, :] = inner[edge : tall - edge, :width]
    out[tall - edge :, :] = inner[tall - edge :, :width] + below
    lane = lax.broadcasted_iota(jnp.int32, (1, LANES), 1)
    left, right = by_parity("skyx", near[...], far[...])
    out[:, :LANES] += jnp.where(lane < margin, left, 0.0)
    out[:, width - LANES :] += jnp.where(lane >= LANES - margin, right, 0.0)


def finish(margin, inner, first, second, near, far):
    tall, wide = inner.shape
    return pl.pallas_call(
        functools.partial(finish_kernel, margin),
        out_shape=jax.ShapeDtypeStruct((tall, wide - LANES), jnp.float32),
        in_specs=[pl.BlockSpec(memory_space=pltpu.VMEM)] * 5,
        out_specs=pl.BlockSpec(memory_space=pltpu.VMEM),
        compiler_params=pltpu.CompilerParams(vmem_limit_bytes=4 << 20),
        name="finish",
    )(inner, first, second, near, far)


def swap(value, axis, first):
    pairs = [(i, i + 1) for i in range(first, lax.axis_size(axis) - 1, 2)]
    return lax.ppermute(value, axis, pairs + [(j, i) for i, j in pairs])


def body(
    image, inverse_var, patch_of, row_of, valid, coef_index, coef_table, basis_across, basis_down
):
    devices = lax.axis_size("skyx") * lax.axis_size("skyy")
    block_count, row_count, block_width = image.shape
    channels = basis_across.shape[0]
    margin = (basis_across.shape[1] - 1) // 2
    patch_rows = RS * row_count
    columns, lines = lax.axis_size("skyx"), lax.axis_size("skyy")
    my_column, my_line = lax.axis_index("skyx"), lax.axis_index("skyy")
    my_patch = my_column * lines + my_line
    patches = patch_of[:, 0]

    weighted = pack(devices, patches, valid, inverse_var, image)
    weighted_in = lax.all_to_all(weighted, BOTH, split_axis=0, concat_axis=0, tiled=True)
    kept = pack(devices, patches, valid, inverse_var)

    choose = (
        coef_index[:, None] == jnp.arange(coef_table.shape[0], dtype=jnp.int32)[None, :]
    ).astype(jnp.float32)
    coeffs = jnp.dot(choose, coef_table, precision=lax.Precision.HIGHEST)
    target_grid = patches.reshape(devices, block_count)
    slot_grid = row_of.reshape(devices, block_count)
    hits = target_grid == my_patch
    slot = jnp.max(jnp.where(hits, slot_grid, -1), axis=1)
    in_slot = slot[None, :] == jnp.arange(RS, dtype=jnp.int32)[:, None]
    one = jnp.where(in_slot[None], coeffs.T[:, None, :], 0.0)
    none = jnp.zeros_like(one)
    table = jnp.concatenate(
        [jnp.concatenate([one, none], axis=2), jnp.concatenate([none, one], axis=2)], axis=1
    ).reshape(channels * 2 * RS, 2 * devices).astype(jnp.bfloat16)
    places = jnp.arange(patch_rows, dtype=jnp.int32)
    edge = (margin + 7) // 8 * 8
    row_at = (places % RS) * row_count + places // RS + edge - margin
    across, down = band_tables(basis_across, basis_down, row_at[None, :], patch_rows + 2 * edge)
    received_rows = jnp.arange(row_count, dtype=jnp.int32)[None, :]
    row_in_patch = jnp.where(slot[:, None] >= 0, slot[:, None] * row_count + received_rows, -1)
    row_in_patch = row_in_patch.reshape(1, devices * row_count)
    kept, table, down, across, row_in_patch = lax.optimization_barrier((kept, table, down, across, row_in_patch))
    kept_in = lax.all_to_all(kept, BOTH, split_axis=0, concat_axis=0, tiled=True)
    down, across = (pltpu.with_memory_space_constraint(x, pltpu.HBM) for x in (down, across))
    inner, first, second = convolve_sum(margin, weighted_in, table, down, across)
    first, second = swap(first, "skyy", 0), swap(second, "skyy", 1)
    side = add_beside(inner, first, second)
    near, far = swap(side, "skyx", 0), swap(side, "skyx", 1)
    weight_sum = place_weights(row_in_patch, kept_in)
    coadd = finish(margin, inner, first, second, near, far)
    return (coadd, weight_sum)


def solution(mesh):
    placed = (P(BOTH, None, None), P(BOTH, None, None), P(), P(), P(), P(), P(), P(), P())
    return jax.shard_map(
        body,
        mesh=mesh,
        in_specs=placed,
        out_specs=(P("skyy", "skyx"), P("skyy", "skyx")),
        check_vma=False,
    )
```

```python
import functools

import jax
import jax.numpy as jnp
from jax import lax
from jax.experimental import pallas as pl
from jax.experimental.pallas import tpu as pltpu
from jax.sharding import PartitionSpec as P

RS = 4
LANES = 128
BOTH = ("skyx", "skyy")


def pack_kernel(planes, patch_of, valid, *refs):
    me = lax.axis_index(BOTH)
    sources, refs = refs[:planes], refs[planes:]
    out, *rooms, packed, targets, usable, arrived, noted, sent = refs
    blocks = rooms[0].shape[0]
    chunks = arrived.shape[1]
    group = blocks // chunks

    def fetch(index, chunk):
        at = pl.ds(chunk * group, group)
        return pltpu.make_async_copy(sources[index].at[at], rooms[index].at[at], arrived.at[index, chunk])

    listed = targets.shape[0]
    devices_listed = listed // blocks
    some = pl.ds(pl.multiple_of(me // devices_listed * listed, listed), listed)
    notes = [
        pltpu.make_async_copy(patch_of.at[some], targets, noted.at[0]),
        pltpu.make_async_copy(valid.at[some], usable, noted.at[1]),
    ]
    for note in notes:
        note.start()
    for chunk in range(chunks):
        for index in range(planes):
            fetch(index, chunk).start()
    unsent = packed.shape[0] - 1
    packed[...] = jnp.zeros_like(packed)
    for note in notes:
        note.wait()
    first = me % devices_listed * blocks
    for chunk in range(chunks):
        for index in range(planes):
            fetch(index, chunk).wait()
        for block in range(chunk * group, chunk * group + group):
            value = rooms[0][block]
            for room in rooms[1:]:
                value = value * room[block]
            place = jnp.where(usable[first + block] != 0, targets[first + block], unsent)
            packed[place] = value
    pieces = sent.shape[0]
    share = unsent // pieces
    copies = []
    for piece in range(pieces):
        at = pl.ds(piece * share, share)
        copies.append(pltpu.make_async_copy(packed.at[at], out.at[at], sent.at[piece]))
        copies[-1].start()
    for copy in copies:
        copy.wait()


def pack(devices, patch_of, valid, *planes):
    blocks, rows, width = planes[0].shape
    chunks, pieces = 2, 2
    return pl.pallas_call(
        functools.partial(pack_kernel, len(planes)),
        out_shape=jax.ShapeDtypeStruct((devices, rows, width), jnp.bfloat16),
        in_specs=[pl.BlockSpec(memory_space=pl.ANY)] * (2 + len(planes)),
        out_specs=pl.BlockSpec(memory_space=pl.ANY),
        scratch_shapes=[pltpu.VMEM((blocks, rows, width), jnp.bfloat16) for _ in planes]
        + [
            pltpu.VMEM((devices + 1, rows, width), jnp.bfloat16),
            pltpu.SMEM((1024,), jnp.int32),
            pltpu.SMEM((1024,), jnp.int32),
            pltpu.SemaphoreType.DMA((len(planes), chunks)),
            pltpu.SemaphoreType.DMA((2,)),
            pltpu.SemaphoreType.DMA((pieces,)),
        ],
        cost_estimate=pl.CostEstimate(
            flops=devices * rows * width,
            bytes_accessed=2 * (len(planes) * blocks + devices) * rows * width,
            transcendentals=0,
        ),
        compiler_params=pltpu.CompilerParams(vmem_limit_bytes=63 << 20),
        name="pack",
    )(patch_of, valid, *planes)


def table_kernel(across_taps, down_taps, row_at, across, down):
    count, ext, places = down.shape
    lane = lax.broadcasted_iota(jnp.int32, (LANES, LANES), 1)
    line = lax.broadcasted_iota(jnp.int32, (LANES, LANES), 0)
    order = (lax.broadcasted_iota(jnp.int32, (LANES, places), 0) == row_at[...]).astype(jnp.bfloat16)
    for c in range(count):
        turned = jnp.broadcast_to(across_taps[c : c + 1, :], (LANES, LANES))
        turned = pltpu.roll(turned, 0, 1, stride=1, stride_axis=0)
        across[c, LANES:, :] = jnp.where(lane >= line, turned, 0.0).astype(jnp.bfloat16)
        across[c, :LANES, :] = jnp.where(lane < line, turned, 0.0).astype(jnp.bfloat16)
        turned = jnp.broadcast_to(down_taps[c : c + 1, :], (LANES, LANES))
        turned = pltpu.roll(turned, 0, 1, stride=1, stride_axis=0)[:ext].astype(jnp.bfloat16)
        down[c] = jnp.dot(turned, order, preferred_element_type=jnp.float32).astype(jnp.bfloat16)


def band_tables(basis_across, basis_down, row_at, ext):
    channels, taps = basis_across.shape
    places = row_at.shape[1]
    across_taps = jnp.pad(basis_across, ((0, 0), (0, LANES - taps)))
    down_taps = jnp.concatenate(
        [basis_down[:, :1], jnp.zeros((channels, LANES - taps), jnp.float32), basis_down[:, :0:-1]], axis=1
    )
    return pl.pallas_call(
        table_kernel,
        out_shape=(
            jax.ShapeDtypeStruct((channels, 2 * LANES, LANES), jnp.bfloat16),
            jax.ShapeDtypeStruct((channels, ext, places), jnp.bfloat16),
        ),
        in_specs=[pl.BlockSpec(memory_space=pltpu.VMEM)] * 3,
        out_specs=(pl.BlockSpec(memory_space=pltpu.VMEM),) * 2,
        compiler_params=pltpu.CompilerParams(vmem_limit_bytes=8 << 20),
        name="band_tables",
    )(across_taps, down_taps, row_at)


def coadd_kernel(
    margin, flux_far, choose, down_far, across_far, inner, first, second,
    flux, down, across, wide, channels, mixed, arrived,
):
    sources, rows, width = flux.shape
    count, ext, _ = down.shape
    pieces = width // LANES
    tiles = pieces + 1
    edge = first.shape[0]
    tall = inner.shape[0]
    chunks = arrived.shape[0] - 2
    share = sources // chunks
    copies = []
    for chunk in range(chunks):
        some = pl.ds(chunk * share, share)
        copies.append(pltpu.make_async_copy(flux_far.at[some], flux.at[some], arrived.at[chunk]))
    copies.append(pltpu.make_async_copy(down_far, down, arrived.at[chunks]))
    copies.append(pltpu.make_async_copy(across_far, across, arrived.at[chunks + 1]))
    for copy in copies:
        copy.start()
    for chunk in range(chunks):
        copies[chunk].wait()
        some = pl.ds(chunk * share, share)
        for piece in range(pieces):
            lanes = pl.ds(piece * LANES, LANES)
            block = flux[some, :, lanes].reshape(share * rows, LANES)
            wide[piece, pl.ds(chunk * share * rows, share * rows), :] = block.astype(jnp.float32)
    table = choose[...]
    for pair in range(rows // 2):
        halves = []
        for half in range(2):
            at = pl.ds(2 * pair + half, sources, stride=rows)
            row = [wide[piece, at, :].astype(jnp.bfloat16) for piece in range(pieces)]
            halves.append(jnp.concatenate(row, axis=1))
        summed = jnp.dot(table, jnp.concatenate(halves, axis=0), preferred_element_type=jnp.float32)
        channels[:, pair * 8 : pair * 8 + 8, :] = summed.reshape(count, 8, width)
    copies[chunks].wait()
    copies[chunks + 1].wait()
    zeros = jnp.zeros((ext, LANES), jnp.bfloat16)
    for c in range(count):
        mixed[c, :, :LANES] = zeros
        mixed[c, :, LANES + width :] = zeros
        mixed[c, :, LANES : LANES + width] = jnp.dot(
            down[c], channels[c].astype(jnp.bfloat16), preferred_element_type=jnp.float32
        ).astype(jnp.bfloat16)
    total = jnp.zeros((tiles * ext, LANES), jnp.float32)
    for c in range(count):
        windows = jnp.concatenate([mixed[c, :, LANES * t : LANES * t + 2 * LANES] for t in range(tiles)], axis=0)
        total = total + jnp.dot(windows, across[c], preferred_element_type=jnp.float32)
    whole = jnp.concatenate([total[t * ext : (t + 1) * ext] for t in range(tiles)], axis=1)
    whole = pltpu.roll(whole, tiles * LANES - margin, 1)
    inner[...] = whole[edge : edge + tall]
    top, bottom = whole[:edge], whole[edge + tall :]
    even = lax.rem(lax.axis_index("skyy"), 2) == 0
    first[...] = jnp.where(even, bottom, top).astype(first.dtype)
    second[...] = jnp.where(even, top, bottom).astype(second.dtype)


def convolve_sum(margin, flux, choose, down, across):
    sources, rows, width = flux.shape
    count, ext, _ = down.shape
    tiles = width // LANES + 1
    tall = RS * rows
    edge = (ext - tall) // 2
    sizes = [(tall, tiles * LANES), (edge, tiles * LANES), (edge, tiles * LANES)]
    types = (jnp.float32, jnp.bfloat16, jnp.bfloat16)
    return pl.pallas_call(
        functools.partial(coadd_kernel, margin),
        out_shape=tuple(jax.ShapeDtypeStruct(*array) for array in zip(sizes, types)),
        in_specs=[
            pl.BlockSpec(memory_space=pltpu.HBM),
            pl.BlockSpec(memory_space=pltpu.VMEM),
            pl.BlockSpec(memory_space=pltpu.HBM),
            pl.BlockSpec(memory_space=pltpu.HBM),
        ],
        out_specs=(pl.BlockSpec(memory_space=pltpu.VMEM),) * len(sizes),
        scratch_shapes=[
            pltpu.VMEM(flux.shape, jnp.bfloat16),
            pltpu.VMEM(down.shape, jnp.bfloat16),
            pltpu.VMEM(across.shape, jnp.bfloat16),
            pltpu.VMEM((width // LANES, sources * rows, LANES), jnp.float32),
            pltpu.VMEM((count, RS * rows, width), jnp.float32),
            pltpu.VMEM((count, ext, (tiles + 1) * LANES), jnp.bfloat16),
            pltpu.SemaphoreType.DMA((4 + 2,)),
        ],
        compiler_params=pltpu.CompilerParams(vmem_limit_bytes=20 << 20),
        cost_estimate=pl.CostEstimate(
            flops=2 * count * ext * tiles * LANES * 2 * LANES,
            bytes_accessed=2 * sources * rows * width + 4 * ext * tiles * LANES,
            transcendentals=0,
        ),
        name="convolve_sum",
    )(flux, choose, down, across)


def weight_kernel(chosen, kept, out):
    sources, rows, width = kept.shape
    out[...] = jnp.dot(chosen[...], kept[...].reshape(sources * rows, width), preferred_element_type=jnp.float32)


def place_weights(chosen, kept):
    sources, rows, width = kept.shape
    return pl.pallas_call(
        weight_kernel,
        out_shape=jax.ShapeDtypeStruct((RS * rows, width), jnp.float32),
        in_specs=[pl.BlockSpec(memory_space=pltpu.VMEM)] * 2,
        out_specs=pl.BlockSpec(memory_space=pltpu.VMEM),
        compiler_params=pltpu.CompilerParams(vmem_limit_bytes=8 << 20),
        cost_estimate=pl.CostEstimate(
            flops=2 * RS * rows * sources * rows * width,
            bytes_accessed=2 * sources * rows * width,
            transcendentals=0,
        ),
        name="place_weights",
    )(chosen, kept)


def by_parity(axis, first, second):
    even = lax.rem(lax.axis_index(axis), 2) == 0
    first, second = first.astype(jnp.float32), second.astype(jnp.float32)
    return jnp.where(even, second, first), jnp.where(even, first, second)


def side_kernel(inner, first, second, out):
    tall, wide = inner.shape
    edge = first.shape[0]
    lanes = slice(wide - LANES, wide)
    above, below = by_parity("skyy", first[:, lanes], second[:, lanes])
    out[:edge, :] = (inner[:edge, lanes] + above).astype(out.dtype)
    out[edge : tall - edge, :] = inner[edge : tall - edge, lanes].astype(out.dtype)
    out[tall - edge :, :] = (inner[tall - edge :, lanes] + below).astype(out.dtype)


def add_beside(inner, first, second):
    return pl.pallas_call(
        side_kernel,
        out_shape=jax.ShapeDtypeStruct((inner.shape[0], LANES), jnp.bfloat16),
        in_specs=[pl.BlockSpec(memory_space=pltpu.VMEM)] * 3,
        out_specs=pl.BlockSpec(memory_space=pltpu.VMEM),
        compiler_params=pltpu.CompilerParams(vmem_limit_bytes=4 << 20),
        name="add_beside",
    )(inner, first, second)


def finish_kernel(margin, inner, first, second, near, far, out):
    tall, width = out.shape
    edge = first.shape[0]
    above, below = by_parity("skyy", first[:, :width], second[:, :width])
    out[:edge, :] = inner[:edge, :width] + above
    out[edge : tall - edge, :] = inner[edge : tall - edge, :width]
    out[tall - edge :, :] = inner[tall - edge :, :width] + below
    lane = lax.broadcasted_iota(jnp.int32, (1, LANES), 1)
    left, right = by_parity("skyx", near[...], far[...])
    out[:, :LANES] += jnp.where(lane < margin, left, 0.0)
    out[:, width - LANES :] += jnp.where(lane >= LANES - margin, right, 0.0)


def finish(margin, inner, first, second, near, far):
    tall, wide = inner.shape
    return pl.pallas_call(
        functools.partial(finish_kernel, margin),
        out_shape=jax.ShapeDtypeStruct((tall, wide - LANES), jnp.float32),
        in_specs=[pl.BlockSpec(memory_space=pltpu.VMEM)] * 5,
        out_specs=pl.BlockSpec(memory_space=pltpu.VMEM),
        compiler_params=pltpu.CompilerParams(vmem_limit_bytes=4 << 20),
        name="finish",
    )(inner, first, second, near, far)


def swap(value, axis, first):
    pairs = [(i, i + 1) for i in range(first, lax.axis_size(axis) - 1, 2)]
    return lax.ppermute(value, axis, pairs + [(j, i) for i, j in pairs])


def body(
    image, inverse_var, patch_of, row_of, valid, coef_index, coef_table, basis_across, basis_down
):
    devices = lax.axis_size("skyx") * lax.axis_size("skyy")
    block_count, row_count, block_width = image.shape
    channels = basis_across.shape[0]
    margin = (basis_across.shape[1] - 1) // 2
    patch_rows = RS * row_count
    columns, lines = lax.axis_size("skyx"), lax.axis_size("skyy")
    my_column, my_line = lax.axis_index("skyx"), lax.axis_index("skyy")
    my_patch = my_column * lines + my_line
    patches = patch_of[:, 0]

    weighted = pack(devices, patches, valid, inverse_var, image)
    weighted_in = lax.all_to_all(weighted, BOTH, split_axis=0, concat_axis=0, tiled=True)
    kept = pack(devices, patches, valid, inverse_var)

    choose = (
        coef_index[:, None] == jnp.arange(coef_table.shape[0], dtype=jnp.int32)[None, :]
    ).astype(jnp.float32)
    coeffs = jnp.dot(choose, coef_table, precision=lax.Precision.HIGHEST)
    target_grid = patches.reshape(devices, block_count)
    slot_grid = row_of.reshape(devices, block_count)
    hits = target_grid == my_patch
    slot = jnp.max(jnp.where(hits, slot_grid, -1), axis=1)
    in_slot = slot[None, :] == jnp.arange(RS, dtype=jnp.int32)[:, None]
    one = jnp.where(in_slot[None], coeffs.T[:, None, :], 0.0)
    none = jnp.zeros_like(one)
    table = jnp.concatenate(
        [jnp.concatenate([one, none], axis=2), jnp.concatenate([none, one], axis=2)], axis=1
    ).reshape(channels * 2 * RS, 2 * devices).astype(jnp.bfloat16)
    places = jnp.arange(patch_rows, dtype=jnp.int32)
    edge = (margin + 7) // 8 * 8
    row_at = (places % RS) * row_count + places // RS + edge - margin
    across, down = band_tables(basis_across, basis_down, row_at[None, :], patch_rows + 2 * edge)
    received_rows = jnp.arange(row_count, dtype=jnp.int32)[None, :]
    row_in_patch = jnp.where(slot[:, None] >= 0, slot[:, None] * row_count + received_rows, -1)
    row_in_patch = row_in_patch.reshape(1, devices * row_count)
    chosen = (places[:, None] == row_in_patch).astype(jnp.bfloat16)
    kept, table, down, across, chosen = lax.optimization_barrier((kept, table, down, across, chosen))
    kept_in = lax.all_to_all(kept, BOTH, split_axis=0, concat_axis=0, tiled=True)
    down, across = (pltpu.with_memory_space_constraint(x, pltpu.HBM) for x in (down, across))
    inner, first, second = convolve_sum(margin, weighted_in, table, down, across)
    first, second = swap(first, "skyy", 0), swap(second, "skyy", 1)
    side = add_beside(inner, first, second)
    near, far = swap(side, "skyx", 0), swap(side, "skyx", 1)
    weight_sum = place_weights(chosen, kept_in)
    coadd = finish(margin, inner, first, second, near, far)
    return (coadd, weight_sum)


def solution(mesh):
    placed = (P(BOTH, None, None), P(BOTH, None, None), P(), P(), P(), P(), P(), P(), P())
    return jax.shard_map(
        body,
        mesh=mesh,
        in_specs=placed,
        out_specs=(P("skyy", "skyx"), P("skyy", "skyx")),
        check_vma=False,
    )
```
